256 devices in a mesh: grp: 16 (over z, core), tp: 16 (over x, y).
Axes of the slice: x: 4, y: 4, z: 8, core: 2. Of those that a mesh axis runs over, the one named last changes fastest.
Arguments:
- tokens: bfloat16 [16384, 8192], P(('grp', 'tp')), may hold values from -6 to 6
- frozen_weight: bfloat16 [8192, 10240], P(None, 'tp'), may hold values from -0.0625 to 0.0625
- down_weight: bfloat16 [64, 64, 8192], P('grp', None, 'tp'), may hold values from -0.0625 to 0.0625
- up_weight: bfloat16 [64, 64, 10240], P('grp', None, 'tp'), may hold values from -0.75 to 0.75
- adapter_storage_slot: int32 [64], replicated, may hold values from 0 to 63, as said below
- adapter_of_block: int32 [128], replicated, may hold values from 0 to 63, as said below
Outputs:
- qkv: bfloat16 [16384, 10240], P('grp', 'tp')
The draws below stay inside these ranges and needn't reach their ends.
Inputs may be any that keep to these rules, and one draw needn't show every extreme that they name: `adapter_storage_slot`: each slot is named by exactly one adapter; an adapter with slot s is stored by group s // 4. `adapter_of_block`: the 8 blocks of one group, blocks g * 8 to (g + 1) * 8 - 1, name adapters stored by 8 different groups.
All inputs are finite; a program needn't handle non-finite values.
Results may differ from the reference program's by a relative error of at most 0.0029.
Values may be sent and summed in bfloat16 or wider, within the bound.
A program may use at most 128 MiB of HBM per device.

```python
import jax
import jax.numpy as jnp
from jax import lax

MODEL_WIDTH = 8192
ADAPTER_RANK = 64
BLOCK = 128
BLK_GRP = 8
ADP_GRP = 4
QUERY_KEY_VALUE = 10240
ADAPTER_COUNT = 64
BLOCKS = 128
ROWS = 16384


def adapter_plan(key):
    groups = BLOCKS // BLK_GRP
    slot_of = jax.random.permutation(jax.random.fold_in(key, 11), ADAPTER_COUNT).astype(jnp.int32)
    adapter_at = jnp.argsort(slot_of, stable=True).astype(jnp.int32)
    popular = jax.random.permutation(jax.random.fold_in(key, 12), groups).astype(jnp.int32)
    random_part = jax.random.randint(jax.random.fold_in(key, 13), (groups, groups), 0, groups)
    owner_score = (random_part + 2 * popular[None, :]) * groups + jnp.arange(groups, dtype=jnp.int32)[None, :]
    owner_pick = lax.top_k(owner_score, BLK_GRP)[1].astype(jnp.int32)
    local_slot = jax.random.randint(jax.random.fold_in(key, 14), (groups, BLK_GRP), 0, ADP_GRP)
    chosen = jnp.take(adapter_at, (owner_pick * ADP_GRP + local_slot).reshape(-1), axis=0)
    return (slot_of, chosen.astype(jnp.int32))


def draw_adapter_storage_slot(key, part):
    return adapter_plan(key)[0]


def draw_adapter_of_block(key, part):
    return adapter_plan(key)[1]


def shard_levels(own_key, dims, split, smallest, high):
    level, own = 1.0, jax.random.fold_in(own_key, 6)
    for position, parts in split:
        heights = jnp.exp(jax.random.uniform(jax.random.fold_in(own, position), (parts,), jnp.float32, smallest / len(split), high / len(split)))
        level = level * jnp.repeat(heights, dims[position] // parts).reshape([-1 if axis == position else 1 for axis in range(len(dims))])
    return level


def gaussian(stream_key, shape, scale, most, shards=(), held_as=jnp.bfloat16):
    result = jax.random.normal(stream_key, shape, jnp.float32) * scale
    if len(shards) > 0:
        result = shard_levels(stream_key, shape, shards, -0.22, 0.18) * result
    return jnp.clip(result, min=-most, max=most).astype(held_as)


def setup_inputs(seed: int = 0) -> dict:
    streams_of = jax.random.split(jax.random.key(seed), 7)
    tokens = gaussian(streams_of[0], (ROWS, MODEL_WIDTH), 1.0, 6.0, ((0, 256),))
    frozen_weight = gaussian(streams_of[1], (MODEL_WIDTH, QUERY_KEY_VALUE), MODEL_WIDTH ** -0.5, 0.0625, ((1, 16),))
    down_weight = gaussian(streams_of[2], (ADAPTER_COUNT, ADAPTER_RANK, MODEL_WIDTH), MODEL_WIDTH ** -0.5, 0.0625, ((0, 16), (2, 16)))
    up_weight = gaussian(streams_of[3], (ADAPTER_COUNT, ADAPTER_RANK, QUERY_KEY_VALUE), ADAPTER_RANK ** -0.5, 0.75, ((0, 16), (2, 16)))
    adapter_storage_slot = draw_adapter_storage_slot(jax.random.fold_in(streams_of[6], 71), 0)
    adapter_of_block = draw_adapter_of_block(jax.random.fold_in(streams_of[6], 71), 0)
    return {"tokens": tokens, "frozen_weight": frozen_weight, "down_weight": down_weight, "up_weight": up_weight, "adapter_storage_slot": adapter_storage_slot, "adapter_of_block": adapter_of_block}


adapter_scale = 0.5


def reference(tokens, frozen_weight, down_weight, up_weight, adapter_storage_slot, adapter_of_block):
    frozen_rows = jnp.dot(tokens, frozen_weight, preferred_element_type=jnp.float32)
    slot_numbers = jnp.take(adapter_storage_slot, adapter_of_block, axis=0).astype(jnp.int32)
    down_tile = jnp.take(down_weight, slot_numbers, axis=0).astype(jnp.float32)
    up_tile = jnp.take(up_weight, slot_numbers, axis=0).astype(jnp.float32)
    blocks = tokens.reshape(-1, BLOCK, MODEL_WIDTH).astype(jnp.float32)
    shrink = jnp.einsum("bnd,brd->bnr", blocks, down_tile).astype(jnp.bfloat16)
    update_rows = jnp.einsum("bnr,brc->bnc", shrink.astype(jnp.float32), up_tile)
    return (frozen_rows + adapter_scale * update_rows.reshape(frozen_rows.shape)).astype(jnp.bfloat16)
```

```python
import jax
import jax.numpy as jnp
from jax import lax
from jax.experimental import pallas as pl
from jax.experimental.pallas import tpu as pltpu
from jax.sharding import PartitionSpec as P

BLOCK = 128
SIDE = 4
RINGS = 4
SUBS = 4
SCALE = 0.5


def ring_time(x, y, turned):
    major = (1 - turned) * x + turned * y
    return SIDE * major + (x + y) % SIDE


def ring_node(t, turned):
    major = t // SIDE
    minor = (t % SIDE + SIDE - major) % SIDE
    return (1 - turned) * (SIDE * major + minor) + turned * (SIDE * minor + major)


def kernel(
    slot_ref, block_ref, tokens_ref, weight_ref, down_ref, up_ref, out_ref,
    gat, w_v, dn_v, up_v, dn_st, up_st, dn_rc, up_rc, acc, part_st, part_rc, sh_st, sh_all, out_v,
    own_sem, w_sem, ad_sem, ring_send, ring_recv, dn_send, dn_recv, up_send, up_recv,
    part_send, part_recv, sh_send, sh_recv, out_sem,
):
    groups = lax.axis_size("grp")
    members = lax.axis_size("tp")
    g = lax.axis_index("grp")
    m = lax.axis_index("tp")
    x, y = m // SIDE, m % SIDE
    rows = tokens_ref.shape[0]
    chunk = gat.shape[4]
    stored = down_ref.shape[0]
    blocks_here = members * rows // BLOCK
    per_block = BLOCK // rows

    def own_copy(r, j):
        c = r * SUBS + j
        return pltpu.make_async_copy(
            tokens_ref.at[:, pl.ds(c * chunk, chunk)], gat.at[r, j, 0], own_sem.at[r, j]
        )

    def w_copy(r, j):
        start = pl.multiple_of((r * SUBS + j) * chunk, chunk)
        return pltpu.make_async_copy(
            weight_ref.at[pl.ds(start, chunk), :], w_v.at[r, j], w_sem.at[r, j]
        )

    for r in range(RINGS):
        for j in range(SUBS):
            own_copy(r, j).start()
    dn_in = pltpu.make_async_copy(down_ref, dn_v, ad_sem.at[0])
    up_in = pltpu.make_async_copy(up_ref, up_v, ad_sem.at[1])
    dn_in.start()
    up_in.start()
    for j in range(SUBS):
        for r in range(RINGS):
            w_copy(r, j).start()

    barrier = pltpu.get_barrier_semaphore()
    for d in range(1, members):
        pl.semaphore_signal(
            barrier, inc=1, device_id={"tp": (m + d) % members}, device_id_type=pl.DeviceIdType.MESH
        )
    for d in range(1, groups):
        pl.semaphore_signal(
            barrier, inc=1, device_id={"grp": (g + d) % groups}, device_id_type=pl.DeviceIdType.MESH
        )

    times = [ring_time(x, y, r // 2) for r in range(RINGS)]

    def source(r, s):
        step = 1 - 2 * (r % 2)
        return ring_node((times[r] - step * s + members) % members, r // 2)

    nexts = [
        ring_node((times[r] + 1 - 2 * (r % 2) + members) % members, r // 2) for r in range(RINGS)
    ]

    def ring_copy(r, j, s):
        return pltpu.make_async_remote_copy(
            src_ref=gat.at[r, j, s],
            dst_ref=gat.at[r, j, s + 1],
            send_sem=ring_send.at[r],
            recv_sem=ring_recv.at[r, j, s + 1],
            device_id={"tp": nexts[r]},
            device_id_type=pl.DeviceIdType.MESH,
        )

    def ring_arrival(r, j, s):
        return pltpu.make_async_remote_copy(
            src_ref=gat.at[r, j, s],
            dst_ref=gat.at[r, j, s],
            send_sem=ring_send.at[r],
            recv_sem=ring_recv.at[r, j, s],
            device_id={"tp": nexts[r]},
            device_id_type=pl.DeviceIdType.MESH,
        )

    for j in range(SUBS):
        for r in range(RINGS):
            own_copy(r, j).wait()
    pl.semaphore_wait(barrier, members - 1 + groups - 1)
    for j in range(SUBS):
        for r in range(RINGS):
            ring_copy(r, j, 0).start()

    def slot_of(b):
        return slot_ref[block_ref[b]]

    dn_in.wait()
    up_in.wait()

    def stage(q, carry):
        pick = 0
        for i in range(blocks_here):
            slot = slot_of(q * blocks_here + i)
            pick = jnp.where(slot // stored == g, slot % stored, pick)
        dn_st[q] = dn_v[pick]
        up_st[q] = up_v[pick]
        return carry

    lax.fori_loop(0, groups, stage, 0)
    dn_rc[g] = dn_st[g]
    up_rc[g] = up_st[g]

    def panel_copy(st, rc, send, recv, d):
        q = (g + d) % groups
        return pltpu.make_async_remote_copy(
            src_ref=st.at[q],
            dst_ref=rc.at[g],
            send_sem=send.at[d],
            recv_sem=recv.at[d],
            device_id={"grp": q},
            device_id_type=pl.DeviceIdType.MESH,
        )

    def panel_arrival(st, rc, send, recv, d):
        q = (g + groups - d) % groups
        return pltpu.make_async_remote_copy(
            src_ref=st.at[q],
            dst_ref=rc.at[q],
            send_sem=send.at[d],
            recv_sem=recv.at[d],
            device_id={"grp": q},
            device_id_type=pl.DeviceIdType.MESH,
        )

    for d in range(1, groups):
        panel_copy(dn_st, dn_rc, dn_send, dn_recv, d).start()
    for d in range(1, groups):
        panel_copy(up_st, up_rc, up_send, up_recv, d).start()

    acc[...] = jnp.zeros_like(acc)

    my_ring, my_sub = m // SUBS, m % SUBS
    my_turn, my_step = my_ring // 2, 1 - 2 * (my_ring % 2)
    my_time = ring_time(x, y, my_turn)

    def home(s):
        return ring_node((my_time - my_step * s + members) % members, my_turn)

    def part_value(s):
        owner = slot_of(g * blocks_here + home(s) // per_block) // stored
        panel = dn_rc[owner]
        twice = jnp.concatenate([panel, panel], axis=0)
        p = lax.dot_general(
            gat[my_ring, my_sub, s], twice, (((1,), (1,)), ((), ())), preferred_element_type=jnp.float32
        )
        high = p.astype(jnp.bfloat16).astype(jnp.float32)
        lane = lax.broadcasted_iota(jnp.int32, p.shape, 1)
        return jnp.where(lane < p.shape[1] // 2, high, p - high).astype(jnp.bfloat16)

    def part_copy(s):
        return pltpu.make_async_remote_copy(
            src_ref=part_st.at[s],
            dst_ref=part_rc.at[m],
            send_sem=part_send.at[s],
            recv_sem=part_recv.at[m],
            device_id={"tp": home(s)},
            device_id_type=pl.DeviceIdType.MESH,
        )

    def part_arrival(d):
        q = (m + d) % members
        return pltpu.make_async_remote_copy(
            src_ref=part_st.at[0],
            dst_ref=part_rc.at[q],
            send_sem=part_send.at[0],
            recv_sem=part_recv.at[q],
            device_id={"tp": q},
            device_id_type=pl.DeviceIdType.MESH,
        )

    def send_part(s):
        part_st[s] = part_value(s)
        part_copy(s).start()

    def product(r, j, pair):
        lhs = gat[r, j, pl.ds(2 * pair, 2)].reshape(2 * rows, chunk)
        res = jnp.dot(lhs, w_v[r, j], preferred_element_type=jnp.float32)
        for i in range(2):
            at = pl.multiple_of(source(r, 2 * pair + i) * rows, rows)
            acc[pl.ds(at, rows), :] += res[i * rows : (i + 1) * rows]

    def arrive(s, forward):
        def sub(j, carry):
            for r in range(RINGS):
                ring_arrival(r, j, s).wait_recv()
                if forward:
                    ring_copy(r, j, s).start()
            return carry

        return sub

    def arrive_and_multiply(pair, forward):
        step = arrive(2 * pair + 1, forward)

        def sub(j, carry):
            step(j, carry)
            for r in range(RINGS):
                product(r, j, pair)
            return carry

        return sub

    for r in range(RINGS):
        for j in range(SUBS):
            w_copy(r, j).wait()
    lax.fori_loop(0, SUBS, arrive_and_multiply(0, True), 0)

    late = 3
    pairs = members // 2

    def middle(pair, carry):
        lax.fori_loop(0, SUBS, arrive(2 * pair, True), 0)
        lax.fori_loop(0, SUBS, arrive_and_multiply(pair, True), 0)
        return carry

    lax.fori_loop(1, late + 1, middle, 0)

    for d in range(1, groups):
        panel_arrival(dn_st, dn_rc, dn_send, dn_recv, d).wait_recv()
    part_rc[m] = part_value(0)

    def early(s, carry):
        send_part(s)
        return carry

    lax.fori_loop(1, 2 * late + 2, early, 0)

    def later(pair, carry):
        middle(pair, carry)
        send_part(2 * pair)
        send_part(2 * pair + 1)
        return carry

    lax.fori_loop(late + 1, pairs - 1, later, 0)

    lax.fori_loop(0, SUBS, arrive(members - 2, True), 0)
    send_part(members - 2)
    lax.fori_loop(0, SUBS, arrive_and_multiply(pairs - 1, False), 0)
    send_part(members - 1)

    def sh_copy(d):
        return pltpu.make_async_remote_copy(
            src_ref=sh_st,
            dst_ref=sh_all.at[m],
            send_sem=sh_send.at[d],
            recv_sem=sh_recv.at[d],
            device_id={"tp": (m + d) % members},
            device_id_type=pl.DeviceIdType.MESH,
        )

    def sh_arrival(d):
        q = (m + members - d) % members
        return pltpu.make_async_remote_copy(
            src_ref=sh_st,
            dst_ref=sh_all.at[q],
            send_sem=sh_send.at[d],
            recv_sem=sh_recv.at[d],
            device_id={"tp": q},
            device_id_type=pl.DeviceIdType.MESH,
        )

    for d in range(1, members):
        part_arrival(d).wait_recv()
    total = part_rc[0].astype(jnp.float32)
    for i in range(1, members):
        total += part_rc[i].astype(jnp.float32)
    half = total.shape[1] // 2
    total += pltpu.roll(total, half, 1)
    shrink = total.astype(jnp.bfloat16)
    sh_st[...] = shrink
    sh_all[m] = shrink
    for d in range(1, members):
        sh_copy(d).start()
    for d in range(1, groups):
        panel_arrival(up_st, up_rc, up_send, up_recv, d).wait_recv()
    for d in range(1, members):
        sh_arrival(d).wait_recv()

    def out_copy(b):
        at = pl.multiple_of(b * BLOCK, BLOCK)
        return pltpu.make_async_copy(
            out_v.at[pl.ds(at, BLOCK), :], out_ref.at[pl.ds(at, BLOCK), :], out_sem.at[b]
        )

    def finish(b, carry):
        owner = slot_of(g * blocks_here + b) // stored
        s = sh_all[pl.ds(per_block * b, per_block)].reshape(BLOCK, 2 * half)[:, :half]
        update = jnp.dot(s, up_rc[owner], preferred_element_type=jnp.float32)
        at = pl.multiple_of(b * BLOCK, BLOCK)
        out_v[pl.ds(at, BLOCK), :] = (acc[pl.ds(at, BLOCK), :] + SCALE * update).astype(out_v.dtype)
        out_copy(b).start()
        return carry

    lax.fori_loop(0, blocks_here, finish, 0)

    for r in range(RINGS):
        whole = gat.at[r, :, pl.ds(0, members - 1)]
        pltpu.make_async_remote_copy(
            src_ref=whole,
            dst_ref=whole,
            send_sem=ring_send.at[r],
            recv_sem=ring_recv.at[r, 0, 0],
            device_id={"tp": nexts[r]},
            device_id_type=pl.DeviceIdType.MESH,
        ).wait_send()
    for d in range(1, groups):
        panel_copy(dn_st, dn_rc, dn_send, dn_recv, d).wait_send()
        panel_copy(up_st, up_rc, up_send, up_recv, d).wait_send()
    for s in range(1, members):
        part_copy(s).wait_send()
        sh_copy(s).wait_send()
    for b in range(blocks_here):
        out_copy(b).wait()


def local(tokens, frozen_weight, down_weight, up_weight, adapter_storage_slot, adapter_of_block):
    groups = lax.axis_size("grp")
    members = lax.axis_size("tp")
    rows, width = tokens.shape
    rank, down_width = down_weight.shape[1:]
    columns = frozen_weight.shape[1]
    chunk = width // (RINGS * SUBS)
    bf16, f32 = jnp.bfloat16, jnp.float32
    any_spec = pl.BlockSpec(memory_space=pl.ANY)
    smem_spec = pl.BlockSpec(memory_space=pltpu.SMEM)
    dma = pltpu.SemaphoreType.DMA
    return pl.pallas_call(
        kernel,
        out_shape=jax.ShapeDtypeStruct((members * rows, columns), bf16),
        in_specs=[smem_spec, smem_spec, any_spec, any_spec, any_spec, any_spec],
        out_specs=any_spec,
        scratch_shapes=[
            pltpu.VMEM((RINGS, SUBS, members, rows, chunk), bf16),
            pltpu.VMEM((RINGS, SUBS, chunk, columns), bf16),
            pltpu.VMEM(down_weight.shape, bf16),
            pltpu.VMEM(up_weight.shape, bf16),
            pltpu.VMEM((groups, rank, down_width), bf16),
            pltpu.VMEM((groups, rank, columns), bf16),
            pltpu.VMEM((groups, rank, down_width), bf16),
            pltpu.VMEM((groups, rank, columns), bf16),
            pltpu.VMEM((members * rows, columns), f32),
            pltpu.VMEM((members, rows, 2 * rank), bf16),
            pltpu.VMEM((members, rows, 2 * rank), bf16),
            pltpu.VMEM((rows, 2 * rank), bf16),
            pltpu.VMEM((members, rows, 2 * rank), bf16),
            pltpu.VMEM((members * rows, columns), bf16),
            dma((RINGS, SUBS)),
            dma((RINGS, SUBS)),
            dma((2,)),
            dma((RINGS,)),
            dma((RINGS, SUBS, members)),
            dma((groups,)),
            dma((groups,)),
            dma((groups,)),
            dma((groups,)),
            dma((members,)),
            dma((members,)),
            dma((members,)),
            dma((members,)),
            dma((members * rows // BLOCK,)),
        ],
        compiler_params=pltpu.CompilerParams(
            collective_id=0, has_side_effects=True, vmem_limit_bytes=60 << 20
        ),
        cost_estimate=pl.CostEstimate(
            flops=2 * members * rows * width * columns,
            bytes_accessed=2 * width * columns + 2 * members * rows * columns,
            transcendentals=0,
        ),
        name="projection",
    )(adapter_storage_slot, adapter_of_block, tokens, frozen_weight, down_weight, up_weight)


def solution(mesh):
    placed = (
        P(("grp", "tp"), None),
        P(None, "tp"),
        P("grp", None, "tp"),
        P("grp", None, "tp"),
        P(),
        P(),
    )
    return jax.shard_map(
        local, mesh=mesh, in_specs=placed, out_specs=P("grp", "tp"), check_vma=False
    )
```

```python
import jax
import jax.numpy as jnp
from jax import lax
from jax.experimental import pallas as pl
from jax.experimental.pallas import tpu as pltpu
from jax.sharding import PartitionSpec as P

BLOCK = 128
CORES = 2
SIDE = 4
RINGS = 4
SUBS = 4
QUARTER = 4
SCALE = 0.5
DIRECT = 2


def ring_time(x, y, turned):
    major = (1 - turned) * x + turned * y
    return SIDE * major + (x + y) % SIDE


def ring_node(t, turned):
    major = t // SIDE
    minor = (t % SIDE + SIDE - major) % SIDE
    return (1 - turned) * (SIDE * major + minor) + turned * (SIDE * minor + major)


def kernel(
    slot_ref, block_ref, tokens_ref, weight_ref, down_ref, up_ref, out_ref,
    gat, w_v, dn_v, up_v, dn_st, up_st, dn_rc, up_rc, acc, part_st, part_rc, sh_st, sh_all, near,
    own_sem, w_sem, ad_sem, ring_send, ring_recv, dn_send, dn_recv, up_send, up_recv,
    part_send, part_recv, sh_send, sh_recv, near_send, near_recv, ready,
):
    groups = lax.axis_size("grp")
    members = lax.axis_size("tp")
    g = lax.axis_index("grp")
    m = lax.axis_index("tp")
    x, y = m // SIDE, m % SIDE
    rows = tokens_ref.shape[0]
    chunk = gat.shape[4]
    stored = down_ref.shape[0]
    blocks_here = members * rows // BLOCK
    per_block = BLOCK // rows

    def own_copy(r, j):
        c = r * SUBS + j
        return pltpu.make_async_copy(
            tokens_ref.at[:, pl.ds(c * chunk, chunk)], gat.at[r, j, 0], own_sem.at[r, j]
        )

    def w_copy(r, j):
        start = pl.multiple_of((r * SUBS + j) * chunk, chunk)
        return pltpu.make_async_copy(
            weight_ref.at[pl.ds(start, chunk), :], w_v.at[r, j], w_sem.at[r, j]
        )

    for r in range(RINGS):
        for j in range(SUBS):
            own_copy(r, j).start()
    dn_in = pltpu.make_async_copy(down_ref, dn_v, ad_sem.at[0])
    up_in = pltpu.make_async_copy(up_ref, up_v, ad_sem.at[1])
    dn_in.start()
    up_in.start()
    for j in range(SUBS):
        for r in range(RINGS):
            w_copy(r, j).start()

    def signal(sem, where):
        pl.semaphore_signal(sem, inc=1, device_id=where, device_id_type=pl.DeviceIdType.MESH)

    other = g + 1 - 2 * (g % CORES)
    barrier = pltpu.get_barrier_semaphore()
    for d in (1, SIDE - 1):
        signal(barrier, {"tp": SIDE * ((x + d) % SIDE) + y})
        signal(barrier, {"tp": SIDE * x + (y + d) % SIDE})
    for d in (CORES, groups - CORES):
        signal(barrier, {"grp": (g + d) % groups})
    signal(barrier, {"grp": other})

    times = [ring_time(x, y, r // 2) for r in range(RINGS)]

    def source(r, s):
        step = 1 - 2 * (r % 2)
        return ring_node((times[r] - step * s + members) % members, r // 2)

    nexts = [
        ring_node((times[r] + 1 - 2 * (r % 2) + members) % members, r // 2) for r in range(RINGS)
    ]

    def ring_copy(r, j, s):
        return pltpu.make_async_remote_copy(
            src_ref=gat.at[r, j, s],
            dst_ref=gat.at[r, j, s + 1],
            send_sem=ring_send.at[r],
            recv_sem=ring_recv.at[r, j, s + 1],
            device_id={"tp": nexts[r]},
            device_id_type=pl.DeviceIdType.MESH,
        )

    def ring_arrival(r, j, s):
        return pltpu.make_async_remote_copy(
            src_ref=gat.at[r, j, s],
            dst_ref=gat.at[r, j, s],
            send_sem=ring_send.at[r],
            recv_sem=ring_recv.at[r, j, s],
            device_id={"tp": nexts[r]},
            device_id_type=pl.DeviceIdType.MESH,
        )

    for j in range(SUBS):
        for r in range(RINGS):
            own_copy(r, j).wait()
    pl.semaphore_wait(barrier, 7)
    for j in range(SUBS):
        for r in range(RINGS):
            ring_copy(r, j, 0).start()

    def slot_of(b):
        return slot_ref[block_ref[b]]

    dn_in.wait()
    up_in.wait()

    def stage(q, carry):
        pick = 0
        for i in range(blocks_here):
            slot = slot_of(q * blocks_here + i)
            pick = jnp.where(slot // stored == g, slot % stored, pick)
        dn_st[q] = dn_v[pick]
        up_st[q] = up_v[pick]
        return carry

    for i in range(2):
        for d in (CORES << i, groups - (CORES << i)):
            signal(ready.at[i], {"grp": (g + d) % groups})
        if i == 0:
            lax.fori_loop(0, groups, stage, 0)
        pl.semaphore_wait(ready.at[i], 2)
    signal(ready.at[2], {"grp": other})
    pl.semaphore_wait(ready.at[2], 1)
    dn_rc[g] = dn_st[g]
    up_rc[g] = up_st[g]

    def panel_copy(st, rc, send, recv, d):
        q = (g + d) % groups
        return pltpu.make_async_remote_copy(
            src_ref=st.at[q],
            dst_ref=rc.at[g],
            send_sem=send.at[d],
            recv_sem=recv.at[d],
            device_id={"grp": q},
            device_id_type=pl.DeviceIdType.MESH,
        )

    def panel_arrival(st, rc, send, recv, d):
        q = (g + groups - d) % groups
        return pltpu.make_async_remote_copy(
            src_ref=st.at[q],
            dst_ref=rc.at[q],
            send_sem=send.at[d],
            recv_sem=recv.at[d],
            device_id={"grp": q},
            device_id_type=pl.DeviceIdType.MESH,
        )

    for d in range(1, groups):
        panel_copy(dn_st, dn_rc, dn_send, dn_recv, d).start()
    for d in range(1, groups):
        panel_copy(up_st, up_rc, up_send, up_recv, d).start()

    acc[...] = jnp.zeros_like(acc)

    my_ring = m // QUARTER

    def piece(r, i, s):
        per_sub = QUARTER // SUBS
        at = pl.multiple_of((i % per_sub) * (chunk // per_sub), chunk // per_sub)
        return gat.at[r, i // per_sub, s, :, pl.ds(at, chunk // per_sub)]

    def my_rows(s):
        return piece(my_ring, m % QUARTER, s)[...]

    my_turn, my_step = my_ring // 2, 1 - 2 * (my_ring % 2)
    my_time = ring_time(x, y, my_turn)

    def home(s):
        return ring_node((my_time - my_step * s + members) % members, my_turn)

    def part_value(s, own_rows):
        owner = slot_of(g * blocks_here + home(s) // per_block) // stored
        panel = dn_rc[owner]
        twice = jnp.concatenate([panel, panel], axis=0)
        p = lax.dot_general(own_rows, twice, (((1,), (1,)), ((), ())), preferred_element_type=jnp.float32)
        lane = lax.broadcasted_iota(jnp.int32, (rows // 2, p.shape[1]), 1)
        return jnp.where(lane < p.shape[1] // 2, p[: rows // 2], p[rows // 2 :])

    def part_copy(s):
        return pltpu.make_async_remote_copy(
            src_ref=part_st.at[s],
            dst_ref=part_rc.at[m],
            send_sem=part_send.at[s],
            recv_sem=part_recv.at[m],
            device_id={"tp": home(s)},
            device_id_type=pl.DeviceIdType.MESH,
        )

    def part_arrival(d):
        q = (m + d) % members
        return pltpu.make_async_remote_copy(
            src_ref=part_st.at[0],
            dst_ref=part_rc.at[q],
            send_sem=part_send.at[0],
            recv_sem=part_recv.at[q],
            device_id={"tp": q},
            device_id_type=pl.DeviceIdType.MESH,
        )

    def send_part(s):
        part_st[s] = part_value(s, my_rows(s))
        part_copy(s).start()

    def near_copy(r, s):
        to = source(r, s)
        return to, pltpu.make_async_remote_copy(
            src_ref=piece(r, to % QUARTER, 0),
            dst_ref=near.at[s - 1],
            send_sem=near_send.at[r, s - 1],
            recv_sem=near_recv.at[s - 1],
            device_id={"tp": to},
            device_id_type=pl.DeviceIdType.MESH,
        )

    def each_near(act):
        for r in range(RINGS):
            for s in range(1, DIRECT + 1):
                to, copy = near_copy(r, s)

                @pl.when(to // QUARTER == r)
                def _():
                    act(copy)

    def near_arrival(s):
        return pltpu.make_async_remote_copy(
            src_ref=near.at[s - 1],
            dst_ref=near.at[s - 1],
            send_sem=near_send.at[0, s - 1],
            recv_sem=near_recv.at[s - 1],
            device_id={"tp": m},
            device_id_type=pl.DeviceIdType.MESH,
        )

    def send_near_part(s):
        far = members - s
        near_arrival(s).wait_recv()
        part_st[far] = part_value(far, near[s - 1])
        part_copy(far).start()

    def product(r, j, pair):
        lhs = gat[r, j, pl.ds(2 * pair, 2)].reshape(2 * rows, chunk)
        res = jnp.dot(lhs, w_v[r, j], preferred_element_type=jnp.float32)
        for i in range(2):
            at = pl.multiple_of(source(r, 2 * pair + i) * rows, rows)
            acc[pl.ds(at, rows), :] += res[i * rows : (i + 1) * rows]

    def arrive(s, forward):
        def sub(j, carry):
            for r in range(RINGS):
                ring_arrival(r, j, s).wait_recv()
                if forward:
                    ring_copy(r, j, s).start()
            return carry

        return sub

    def arrive_and_multiply(pair, forward):
        step = arrive(2 * pair + 1, forward)

        def sub(j, carry):
            step(j, carry)
            for r in range(RINGS):
                product(r, j, pair)
            return carry

        return sub

    for r in range(RINGS):
        for j in range(SUBS):
            w_copy(r, j).wait()
    lax.fori_loop(0, SUBS, arrive_and_multiply(0, True), 0)

    late = 3
    pairs = members // 2

    def middle(pair, carry):
        lax.fori_loop(0, SUBS, arrive(2 * pair, True), 0)
        lax.fori_loop(0, SUBS, arrive_and_multiply(pair, True), 0)
        return carry

    lax.fori_loop(1, DIRECT // 2 + 1, middle, 0)
    each_near(lambda copy: copy.start())
    lax.fori_loop(DIRECT // 2 + 1, late + 1, middle, 0)

    for d in range(1, groups):
        panel_arrival(dn_st, dn_rc, dn_send, dn_recv, d).wait_recv()
    part_rc[m] = part_value(0, my_rows(0))

    def early(s, carry):
        send_part(s)
        return carry

    lax.fori_loop(1, 2 * late + 2, early, 0)
    for s in range(1, DIRECT + 1):
        send_near_part(s)

    def later(pair, carry):
        lax.fori_loop(0, SUBS, arrive(2 * pair, True), 0)

        @pl.when(2 * pair < members - DIRECT)
        def _():
            send_part(2 * pair)

        lax.fori_loop(0, SUBS, arrive_and_multiply(pair, True), 0)

        @pl.when(2 * pair + 1 < members - DIRECT)
        def _():
            send_part(2 * pair + 1)

        return carry

    lax.fori_loop(late + 1, pairs - 1, later, 0)
    lax.fori_loop(0, SUBS, arrive(members - 2, True), 0)

    def sh_copy(d):
        return pltpu.make_async_remote_copy(
            src_ref=sh_st,
            dst_ref=sh_all.at[m],
            send_sem=sh_send.at[d],
            recv_sem=sh_recv.at[d],
            device_id={"tp": (m + d) % members},
            device_id_type=pl.DeviceIdType.MESH,
        )

    def sh_arrival(d):
        q = (m + members - d) % members
        return pltpu.make_async_remote_copy(
            src_ref=sh_st,
            dst_ref=sh_all.at[q],
            send_sem=sh_send.at[d],
            recv_sem=sh_recv.at[d],
            device_id={"tp": q},
            device_id_type=pl.DeviceIdType.MESH,
        )

    for d in range(1, members):
        part_arrival(d).wait_recv()
    total = part_rc[0]
    for i in range(1, members):
        total += part_rc[i]
    shrink = total.astype(jnp.bfloat16)
    sh_st[...] = shrink
    sh_all[m] = shrink
    for d in range(1, members):
        sh_copy(d).start()
    lax.fori_loop(0, SUBS, arrive_and_multiply(pairs - 1, False), 0)
    for d in range(1, groups):
        panel_arrival(up_st, up_rc, up_send, up_recv, d).wait_recv()
    for d in range(1, members):
        sh_arrival(d).wait_recv()

    def finish(b, carry):
        owner = slot_of(g * blocks_here + b) // stored
        packed = [sh_all[per_block * b + i].astype(jnp.float32) for i in range(per_block)]
        lane = lax.broadcasted_iota(jnp.int32, packed[0].shape, 1)
        low = lane < packed[0].shape[1] // 2
        split = [jnp.where(low == first, p, 0.0) for p in packed for first in (True, False)]
        s = jnp.concatenate(split, axis=0).astype(jnp.bfloat16)
        panel = up_rc[owner]
        twice = jnp.concatenate([panel, panel], axis=0)
        update = jnp.dot(s, twice, preferred_element_type=jnp.float32)
        at = pl.multiple_of(b * BLOCK, BLOCK)
        out_ref[pl.ds(at, BLOCK), :] = (acc[pl.ds(at, BLOCK), :] + SCALE * update).astype(out_ref.dtype)
        return carry

    lax.fori_loop(0, blocks_here, finish, 0)

    for r in range(RINGS):
        whole = gat.at[r, :, pl.ds(0, members - 1)]
        pltpu.make_async_remote_copy(
            src_ref=whole,
            dst_ref=whole,
            send_sem=ring_send.at[r],
            recv_sem=ring_recv.at[r, 0, 0],
            device_id={"tp": nexts[r]},
            device_id_type=pl.DeviceIdType.MESH,
        ).wait_send()
    for d in range(1, groups):
        panel_copy(dn_st, dn_rc, dn_send, dn_recv, d).wait_send()
        panel_copy(up_st, up_rc, up_send, up_recv, d).wait_send()
    for s in range(1, members):
        part_copy(s).wait_send()
        sh_copy(s).wait_send()
    each_near(lambda copy: copy.wait_send())


def local(tokens, frozen_weight, down_weight, up_weight, adapter_storage_slot, adapter_of_block):
    groups = lax.axis_size("grp")
    members = lax.axis_size("tp")
    rows, width = tokens.shape
    rank, down_width = down_weight.shape[1:]
    columns = frozen_weight.shape[1]
    chunk = width // (RINGS * SUBS)
    bf16, f32 = jnp.bfloat16, jnp.float32
    hbm_spec = pl.BlockSpec(memory_space=pltpu.HBM)
    smem_spec = pl.BlockSpec(memory_space=pltpu.SMEM)
    dma = pltpu.SemaphoreType.DMA
    return pl.pallas_call(
        kernel,
        out_shape=jax.ShapeDtypeStruct((members * rows, columns), bf16),
        in_specs=[smem_spec, smem_spec, hbm_spec, hbm_spec, hbm_spec, hbm_spec],
        out_specs=pl.BlockSpec(memory_space=pltpu.VMEM),
        scratch_shapes=[
            pltpu.VMEM((RINGS, SUBS, members, rows, chunk), bf16),
            pltpu.VMEM((RINGS, SUBS, chunk, columns), bf16),
            pltpu.VMEM(down_weight.shape, bf16),
            pltpu.VMEM(up_weight.shape, bf16),
            pltpu.VMEM((groups, rank, down_width), bf16),
            pltpu.VMEM((groups, rank, columns), bf16),
            pltpu.VMEM((groups, rank, down_width), bf16),
            pltpu.VMEM((groups, rank, columns), bf16),
            pltpu.VMEM((members * rows, columns), f32),
            pltpu.VMEM((members, rows // 2, 2 * rank), f32),
            pltpu.VMEM((members, rows // 2, 2 * rank), f32),
            pltpu.VMEM((rows // 2, 2 * rank), bf16),
            pltpu.VMEM((members, rows // 2, 2 * rank), bf16),
            pltpu.VMEM((DIRECT, rows, down_width), bf16),
            dma((RINGS, SUBS)),
            dma((RINGS, SUBS)),
            dma((2,)),
            dma((RINGS,)),
            dma((RINGS, SUBS, members)),
            dma((groups,)),
            dma((groups,)),
            dma((groups,)),
            dma((groups,)),
            dma((members,)),
            dma((members,)),
            dma((members,)),
            dma((members,)),
            dma((RINGS, DIRECT)),
            dma((DIRECT,)),
            pltpu.SemaphoreType.REGULAR((3,)),
        ],
        compiler_params=pltpu.CompilerParams(
            collective_id=0, has_side_effects=True, vmem_limit_bytes=42 << 20
        ),
        cost_estimate=pl.CostEstimate(
            flops=2 * members * rows * width * columns,
            bytes_accessed=2 * width * columns + 2 * members * rows * columns,
            transcendentals=0,
        ),
        name="projection",
    )(adapter_storage_slot, adapter_of_block, *[pltpu.with_memory_space_constraint(a, pltpu.HBM) for a in (tokens, frozen_weight, down_weight, up_weight)])


def solution(mesh):
    placed = (
        P(("grp", "tp"), None),
        P(None, "tp"),
        P("grp", None, "tp"),
        P("grp", None, "tp"),
        P(),
        P(),
    )
    return jax.shard_map(
        local, mesh=mesh, in_specs=placed, out_specs=P("grp", "tp"), check_vma=False
    )
```

```python
import jax
import jax.numpy as jnp
from jax import lax
from jax.experimental import pallas as pl
from jax.experimental.pallas import tpu as pltpu
from jax.sharding import PartitionSpec as P

BLOCK = 128
CORES = 2
SIDE = 4
RINGS = 4
SUBS = 4
SCALE = 0.5
CHUNKS = RINGS * SUBS
EARLY = 8


def ring_time(x, y, turned):
    major = (1 - turned) * x + turned * y
    return SIDE * major + (x + y) % SIDE


def ring_node(t, turned):
    major = t // SIDE
    minor = (t % SIDE + SIDE - major) % SIDE
    return (1 - turned) * (SIDE * major + minor) + turned * (SIDE * minor + major)


RIDES = ((378, 53229, 18521, 15202), (6059, 53229, 22822, 33795), (10155, 53229, 25348, 38168), (15032, 53229, 1045, 30249))
CARRIERS = ((64547, 7579, 57482, 25927), (51517, 10430, 431, 25927), (41945, 11240, 508, 25927), (15771, 65162, 4800, 25927))


def pick(table, index):
    value = table[0]
    for i in range(1, len(table)):
        value = jnp.where(index == i, table[i], value)
    return value


def feature(member, r, j):
    x, y = member // SIDE, member % SIDE
    k = lax.shift_right_logical(pick([row[r] for row in RIDES], (x + y) % SIDE), 4 * j) % CHUNKS
    return SIDE * ((k // SIDE + x) % SIDE) + (k % SIDE + SIDE - x) % SIDE


def carrier(member, chunk):
    x, y = member // SIDE, member % SIDE
    i, k = (chunk // SIDE + SIDE - x) % SIDE, (chunk % SIDE + x) % SIDE
    entry = pick([pick(row, i) for row in CARRIERS], (x + y) % SIDE)
    at = lax.shift_right_logical(entry, 4 * k) % CHUNKS
    return at // SUBS, at % SUBS


def kernel(
    slot_ref, block_ref, tokens_ref, weight_ref, down_ref, up_ref, out_ref,
    gat, w_v, dn_v, up_v, dn_st, up_st, dn_rc, up_rc, acc, part_st, part_rc, sh_st, sh_all,
    own_sem, w_sem, ad_sem, ring_send, ring_recv, dn_send, dn_recv, up_send, up_recv,
    part_send, part_recv, sh_send, sh_recv, ready,
):
    groups = lax.axis_size("grp")
    members = lax.axis_size("tp")
    g = lax.axis_index("grp")
    m = lax.axis_index("tp")
    x, y = m // SIDE, m % SIDE
    rows = tokens_ref.shape[0]
    chunk = gat.shape[4]
    stored = down_ref.shape[0]
    blocks_here = members * rows // BLOCK
    per_block = BLOCK // rows

    def own_copy(r, j):
        start = pl.multiple_of(feature(m, r, j) * chunk, chunk)
        return pltpu.make_async_copy(
            tokens_ref.at[:, pl.ds(start, chunk)], gat.at[r, j, 0], own_sem.at[r, j]
        )

    def w_copy(c):
        return pltpu.make_async_copy(weight_ref.at[pl.ds(c * chunk, chunk), :], w_v.at[c], w_sem.at[c])

    for r in range(RINGS):
        for j in range(SUBS):
            own_copy(r, j).start()
    dn_in = pltpu.make_async_copy(down_ref, dn_v, ad_sem.at[0])
    up_in = pltpu.make_async_copy(up_ref, up_v, ad_sem.at[1])
    dn_in.start()
    up_in.start()
    for c in range(CHUNKS):
        w_copy(c).start()

    def signal(sem, where):
        pl.semaphore_signal(sem, inc=1, device_id=where, device_id_type=pl.DeviceIdType.MESH)

    other = g + 1 - 2 * (g % CORES)
    barrier = pltpu.get_barrier_semaphore()
    for d in (1, SIDE - 1):
        signal(barrier, {"tp": SIDE * ((x + d) % SIDE) + y})
        signal(barrier, {"tp": SIDE * x + (y + d) % SIDE})
    for d in (CORES, groups - CORES):
        signal(barrier, {"grp": (g + d) % groups})
    signal(barrier, {"grp": other})

    times = [ring_time(x, y, r // 2) for r in range(RINGS)]

    def source(r, s):
        step = 1 - 2 * (r % 2)
        return ring_node((times[r] - step * s + members) % members, r // 2)

    nexts = [
        ring_node((times[r] + 1 - 2 * (r % 2) + members) % members, r // 2) for r in range(RINGS)
    ]

    def ring_copy(r, j, s):
        return pltpu.make_async_remote_copy(
            src_ref=gat.at[r, j, s],
            dst_ref=gat.at[r, j, s + 1],
            send_sem=ring_send.at[r],
            recv_sem=ring_recv.at[r, j, s + 1],
            device_id={"tp": nexts[r]},
            device_id_type=pl.DeviceIdType.MESH,
        )

    def ring_arrival(r, j, s):
        return pltpu.make_async_remote_copy(
            src_ref=gat.at[r, j, s],
            dst_ref=gat.at[r, j, s],
            send_sem=ring_send.at[r],
            recv_sem=ring_recv.at[r, j, s],
            device_id={"tp": nexts[r]},
            device_id_type=pl.DeviceIdType.MESH,
        )

    for j in range(SUBS):
        for r in range(RINGS):
            own_copy(r, j).wait()
    pl.semaphore_wait(barrier, 7)
    for j in range(SUBS):
        for r in range(RINGS):
            ring_copy(r, j, 0).start()

    def slot_of(b):
        return slot_ref[block_ref[b]]

    dn_in.wait()
    up_in.wait()

    def stage(q, carry):
        pick = 0
        for i in range(blocks_here):
            slot = slot_of(q * blocks_here + i)
            pick = jnp.where(slot // stored == g, slot % stored, pick)
        dn_st[q] = dn_v[pick]
        up_st[q] = up_v[pick]
        return carry

    for i in range(2):
        for d in (CORES << i, groups - (CORES << i)):
            signal(ready.at[i], {"grp": (g + d) % groups})
        if i == 0:
            lax.fori_loop(0, groups, stage, 0)
        pl.semaphore_wait(ready.at[i], 2)
    signal(ready.at[2], {"grp": other})
    pl.semaphore_wait(ready.at[2], 1)
    dn_rc[g] = dn_st[g]
    up_rc[g] = up_st[g]

    def panel_copy(st, rc, send, recv, d):
        q = (g + d) % groups
        return pltpu.make_async_remote_copy(
            src_ref=st.at[q],
            dst_ref=rc.at[g],
            send_sem=send.at[d],
            recv_sem=recv.at[d],
            device_id={"grp": q},
            device_id_type=pl.DeviceIdType.MESH,
        )

    def panel_arrival(st, rc, send, recv, d):
        q = (g + groups - d) % groups
        return pltpu.make_async_remote_copy(
            src_ref=st.at[q],
            dst_ref=rc.at[q],
            send_sem=send.at[d],
            recv_sem=recv.at[d],
            device_id={"grp": q},
            device_id_type=pl.DeviceIdType.MESH,
        )

    for d in range(1, groups):
        panel_copy(dn_st, dn_rc, dn_send, dn_recv, d).start()
    for d in range(1, groups):
        panel_copy(up_st, up_rc, up_send, up_recv, d).start()

    acc[...] = jnp.zeros_like(acc)

    def part_value(q, ring, sub, s):
        owner = slot_of(g * blocks_here + q // per_block) // stored
        panel = dn_rc[owner]
        twice = jnp.concatenate([panel, panel], axis=0)
        p = lax.dot_general(
            gat[ring, sub, s], twice, (((1,), (1,)), ((), ())), preferred_element_type=jnp.float32
        )
        lane = lax.broadcasted_iota(jnp.int32, (rows // 2, p.shape[1]), 1)
        return jnp.where(lane < p.shape[1] // 2, p[: rows // 2], p[rows // 2 :])

    def part_copy(d):
        return pltpu.make_async_remote_copy(
            src_ref=part_st.at[d],
            dst_ref=part_rc.at[m],
            send_sem=part_send.at[d],
            recv_sem=part_recv.at[m],
            device_id={"tp": (m + d) % members},
            device_id_type=pl.DeviceIdType.MESH,
        )

    def part_arrival(d):
        q = (m + d) % members
        return pltpu.make_async_remote_copy(
            src_ref=part_st.at[0],
            dst_ref=part_rc.at[q],
            send_sem=part_send.at[0],
            recv_sem=part_recv.at[q],
            device_id={"tp": q},
            device_id_type=pl.DeviceIdType.MESH,
        )

    def my_part(d):
        q = (m + d) % members
        ring, sub = carrier(q, m)
        turned, step = ring // 2, 1 - 2 * (ring % 2)
        s = (step * (ring_time(x, y, turned) - ring_time(q // SIDE, q % SIDE, turned)) + members) % members
        return part_value(q, ring, sub, s)

    def send_part(d):
        part_st[d] = my_part(d)
        part_copy(d).start()

    def add(r, s, value):
        at = pl.multiple_of(source(r, s) * rows, rows)
        acc[pl.ds(at, rows), :] += value

    def product(r, j, s):
        w = w_v[feature(source(r, s), r, j)]
        return jnp.dot(gat[r, j, s], w, preferred_element_type=jnp.float32)

    def multiply(r, s):
        total = product(r, 0, s)
        for j in range(1, SUBS):
            total += product(r, j, s)
        add(r, s, total)

    def phase(j, s, forward=True):
        for r in range(RINGS):
            ring_arrival(r, j, s).wait_recv()
            if forward:
                ring_copy(r, j, s).start()
        for r in range(RINGS):

            @pl.when(j == r)
            def _():
                multiply(r, s - 1)

    def plain_step(s, carry):
        def sub(j, c):
            phase(j, s)
            return c

        lax.fori_loop(0, SUBS, sub, 0)
        return carry

    def part_step(s, carry):
        def sub(j, c):
            phase(j, s)
            for i in range(2):
                d = 1 + 2 * SUBS * (s - EARLY - 1) + 2 * j + i

                @pl.when(d < members)
                def _():
                    send_part(d)

            return c

        lax.fori_loop(0, SUBS, sub, 0)
        return carry

    for c in range(CHUNKS):
        w_copy(c).wait()
    lax.fori_loop(1, EARLY + 1, plain_step, 0)
    for d in range(1, groups):
        panel_arrival(dn_st, dn_rc, dn_send, dn_recv, d).wait_recv()
    part_rc[m] = my_part(0)
    lax.fori_loop(EARLY + 1, EARLY + 3, part_step, 0)
    lax.fori_loop(EARLY + 3, EARLY + 5, plain_step, 0)

    def sh_copy(d):
        return pltpu.make_async_remote_copy(
            src_ref=sh_st,
            dst_ref=sh_all.at[m],
            send_sem=sh_send.at[d],
            recv_sem=sh_recv.at[d],
            device_id={"tp": (m + d) % members},
            device_id_type=pl.DeviceIdType.MESH,
        )

    def sh_arrival(d):
        q = (m + members - d) % members
        return pltpu.make_async_remote_copy(
            src_ref=sh_st,
            dst_ref=sh_all.at[q],
            send_sem=sh_send.at[d],
            recv_sem=sh_recv.at[d],
            device_id={"tp": q},
            device_id_type=pl.DeviceIdType.MESH,
        )

    for d in range(1, members):
        part_arrival(d).wait_recv()
    total = part_rc[0]
    for i in range(1, members):
        total += part_rc[i]
    shrink = total.astype(jnp.bfloat16)
    sh_st[...] = shrink
    sh_all[m] = shrink
    for d in range(1, members):
        sh_copy(d).start()
    lax.fori_loop(EARLY + 5, members - 2, plain_step, 0)

    def update(b):
        owner = slot_of(g * blocks_here + b) // stored
        packed = [sh_all[per_block * b + i].astype(jnp.float32) for i in range(per_block)]
        lane = lax.broadcasted_iota(jnp.int32, packed[0].shape, 1)
        low = lane < packed[0].shape[1] // 2
        split = [jnp.where(low == first, p, 0.0) for p in packed for first in (True, False)]
        s = jnp.concatenate(split, axis=0).astype(jnp.bfloat16)
        panel = up_rc[owner]
        twice = jnp.concatenate([panel, panel], axis=0)
        value = jnp.dot(s, twice, preferred_element_type=jnp.float32)
        at = pl.multiple_of(b * BLOCK, BLOCK)
        acc[pl.ds(at, BLOCK), :] += SCALE * value

    def before_last(j, carry):
        phase(j, members - 2)
        return carry

    def before_last_update(j, carry):
        phase(j, members - 2)
        share = blocks_here // (SUBS // 2)
        lax.fori_loop(0, share, lambda i, c: (update(share * (j - SUBS // 2) + i), c)[1], 0)
        return carry

    lax.fori_loop(0, SUBS // 2, before_last, 0)
    for d in range(1, groups):
        panel_arrival(up_st, up_rc, up_send, up_recv, d).wait_recv()
    for d in range(1, members):
        sh_arrival(d).wait_recv()
    lax.fori_loop(SUBS // 2, SUBS, before_last_update, 0)

    def last(j, carry):
        phase(j, members - 1, forward=False)
        for r in range(RINGS):
            add(r, members - 1, product(r, j, members - 1))
        return carry

    lax.fori_loop(0, SUBS, last, 0)

    def finish(b, carry):
        at = pl.multiple_of(b * BLOCK, BLOCK)
        out_ref[pl.ds(at, BLOCK), :] = acc[pl.ds(at, BLOCK), :].astype(out_ref.dtype)
        return carry

    lax.fori_loop(0, blocks_here, finish, 0)

    for r in range(RINGS):
        whole = gat.at[r, :, pl.ds(0, members - 1)]
        pltpu.make_async_remote_copy(
            src_ref=whole,
            dst_ref=whole,
            send_sem=ring_send.at[r],
            recv_sem=ring_recv.at[r, 0, 0],
            device_id={"tp": nexts[r]},
            device_id_type=pl.DeviceIdType.MESH,
        ).wait_send()
    for d in range(1, groups):
        panel_copy(dn_st, dn_rc, dn_send, dn_recv, d).wait_send()
        panel_copy(up_st, up_rc, up_send, up_recv, d).wait_send()
    for s in range(1, members):
        part_copy(s).wait_send()
        sh_copy(s).wait_send()


def local(tokens, frozen_weight, down_weight, up_weight, adapter_storage_slot, adapter_of_block):
    groups = lax.axis_size("grp")
    members = lax.axis_size("tp")
    rows, width = tokens.shape
    rank, down_width = down_weight.shape[1:]
    columns = frozen_weight.shape[1]
    chunk = width // (RINGS * SUBS)
    bf16, f32 = jnp.bfloat16, jnp.float32
    hbm_spec = pl.BlockSpec(memory_space=pltpu.HBM)
    smem_spec = pl.BlockSpec(memory_space=pltpu.SMEM)
    dma = pltpu.SemaphoreType.DMA
    return pl.pallas_call(
        kernel,
        out_shape=jax.ShapeDtypeStruct((members * rows, columns), bf16),
        in_specs=[smem_spec, smem_spec, hbm_spec, hbm_spec, hbm_spec, hbm_spec],
        out_specs=pl.BlockSpec(memory_space=pltpu.VMEM),
        scratch_shapes=[
            pltpu.VMEM((RINGS, SUBS, members, rows, chunk), bf16),
            pltpu.VMEM((CHUNKS, chunk, columns), bf16),
            pltpu.VMEM(down_weight.shape, bf16),
            pltpu.VMEM(up_weight.shape, bf16),
            pltpu.VMEM((groups, rank, down_width), bf16),
            pltpu.VMEM((groups, rank, columns), bf16),
            pltpu.VMEM((groups, rank, down_width), bf16),
            pltpu.VMEM((groups, rank, columns), bf16),
            pltpu.VMEM((members * rows, columns), f32),
            pltpu.VMEM((members, rows // 2, 2 * rank), f32),
            pltpu.VMEM((members, rows // 2, 2 * rank), f32),
            pltpu.VMEM((rows // 2, 2 * rank), bf16),
            pltpu.VMEM((members, rows // 2, 2 * rank), bf16),
            dma((RINGS, SUBS)),
            dma((CHUNKS,)),
            dma((2,)),
            dma((RINGS,)),
            dma((RINGS, SUBS, members)),
            dma((groups,)),
            dma((groups,)),
            dma((groups,)),
            dma((groups,)),
            dma((members,)),
            dma((members,)),
            dma((members,)),
            dma((members,)),
            pltpu.SemaphoreType.REGULAR((3,)),
        ],
        compiler_params=pltpu.CompilerParams(
            collective_id=0, has_side_effects=True, vmem_limit_bytes=42 << 20
        ),
        cost_estimate=pl.CostEstimate(
            flops=2 * members * rows * width * columns,
            bytes_accessed=2 * width * columns + 2 * members * rows * columns,
            transcendentals=0,
        ),
        name="projection",
    )(adapter_storage_slot, adapter_of_block, *[pltpu.with_memory_space_constraint(a, pltpu.HBM) for a in (tokens, frozen_weight, down_weight, up_weight)])


def solution(mesh):
    placed = (
        P(("grp", "tp"), None),
        P(None, "tp"),
        P("grp", None, "tp"),
        P("grp", None, "tp"),
        P(),
        P(),
    )
    return jax.shard_map(
        local, mesh=mesh, in_specs=placed, out_specs=P("grp", "tp"), check_vma=False
    )
```

```python
import jax
import jax.numpy as jnp
from jax import lax
from jax.experimental import pallas as pl
from jax.experimental.pallas import tpu as pltpu
from jax.sharding import PartitionSpec as P

BLOCK = 128
CORES = 2
SIDE = 4
RINGS = 4
SUBS = 4
SCALE = 0.5
CHUNKS = RINGS * SUBS
EARLY = 8


def ring_time(x, y, turned):
    major = (1 - turned) * x + turned * y
    return SIDE * major + (x + y) % SIDE


def ring_node(t, turned):
    major = t // SIDE
    minor = (t % SIDE + SIDE - major) % SIDE
    return (1 - turned) * (SIDE * major + minor) + turned * (SIDE * minor + major)


RIDES = ((378, 53229, 18521, 15202), (6059, 53229, 22822, 33795), (10155, 53229, 25348, 38168), (15032, 53229, 1045, 30249))
CARRIERS = ((64547, 7579, 57482, 25927), (51517, 10430, 431, 25927), (41945, 11240, 508, 25927), (15771, 65162, 4800, 25927))


def pick(table, index):
    value = table[0]
    for i in range(1, len(table)):
        value = jnp.where(index == i, table[i], value)
    return value


def feature(member, r, j):
    x, y = member // SIDE, member % SIDE
    k = lax.shift_right_logical(pick([row[r] for row in RIDES], (x + y) % SIDE), 4 * j) % CHUNKS
    return SIDE * ((k // SIDE + x) % SIDE) + (k % SIDE + SIDE - x) % SIDE


def carrier(member, chunk):
    x, y = member // SIDE, member % SIDE
    i, k = (chunk // SIDE + SIDE - x) % SIDE, (chunk % SIDE + x) % SIDE
    entry = pick([pick(row, i) for row in CARRIERS], (x + y) % SIDE)
    at = lax.shift_right_logical(entry, 4 * k) % CHUNKS
    return at // SUBS, at % SUBS


def kernel(
    slot_in, block_in, tokens_ref, weight_ref, down_ref, up_ref, out_ref,
    slot_ref, block_ref, gat, w_v, dn_v, up_v, dn_st, up_st, dn_rc, up_rc, acc, part_st, part_rc, sh_st, sh_all,
    own_sem, w_sem, ad_sem, ring_send, ring_recv, dn_send, dn_recv, up_send, up_recv,
    part_send, part_recv, sh_send, sh_recv, ready,
):
    groups = lax.axis_size("grp")
    members = lax.axis_size("tp")
    g = lax.axis_index("grp")
    m = lax.axis_index("tp")
    x, y = m // SIDE, m % SIDE
    rows = tokens_ref.shape[0]
    chunk = gat.shape[4]
    stored = down_ref.shape[0]
    blocks_here = members * rows // BLOCK
    per_block = BLOCK // rows

    def own_copy(r, j):
        start = pl.multiple_of(feature(m, r, j) * chunk, chunk)
        return pltpu.make_async_copy(
            tokens_ref.at[:, pl.ds(start, chunk)], gat.at[r, j, 0], own_sem.at[r, j]
        )

    def w_copy(c):
        return pltpu.make_async_copy(weight_ref.at[pl.ds(c * chunk, chunk), :], w_v.at[c], w_sem.at[c])

    for r in range(RINGS):
        for j in range(SUBS):
            own_copy(r, j).start()
    dn_in = pltpu.make_async_copy(down_ref, dn_v, ad_sem.at[0])
    up_in = pltpu.make_async_copy(up_ref, up_v, ad_sem.at[1])
    slot_copy = pltpu.make_async_copy(slot_in, slot_ref, ad_sem.at[2])
    block_copy = pltpu.make_async_copy(block_in, block_ref, ad_sem.at[3])
    dn_in.start()
    up_in.start()
    slot_copy.start()
    block_copy.start()
    for c in range(CHUNKS):
        w_copy(c).start()

    def signal(sem, where):
        pl.semaphore_signal(sem, inc=1, device_id=where, device_id_type=pl.DeviceIdType.MESH)

    other = g + 1 - 2 * (g % CORES)
    barrier = pltpu.get_barrier_semaphore()
    for d in (1, SIDE - 1):
        signal(barrier, {"tp": SIDE * ((x + d) % SIDE) + y})
        signal(barrier, {"tp": SIDE * x + (y + d) % SIDE})
    for d in (CORES, groups - CORES):
        signal(barrier, {"grp": (g + d) % groups})
    signal(barrier, {"grp": other})

    times = [ring_time(x, y, r // 2) for r in range(RINGS)]

    def source(r, s):
        step = 1 - 2 * (r % 2)
        return ring_node((times[r] - step * s + members) % members, r // 2)

    nexts = [
        ring_node((times[r] + 1 - 2 * (r % 2) + members) % members, r // 2) for r in range(RINGS)
    ]

    def ring_copy(r, j, s):
        return pltpu.make_async_remote_copy(
            src_ref=gat.at[r, j, s],
            dst_ref=gat.at[r, j, s + 1],
            send_sem=ring_send.at[r],
            recv_sem=ring_recv.at[r, j, s + 1],
            device_id={"tp": nexts[r]},
            device_id_type=pl.DeviceIdType.MESH,
        )

    def ring_arrival(r, j, s):
        return pltpu.make_async_remote_copy(
            src_ref=gat.at[r, j, s],
            dst_ref=gat.at[r, j, s],
            send_sem=ring_send.at[r],
            recv_sem=ring_recv.at[r, j, s],
            device_id={"tp": nexts[r]},
            device_id_type=pl.DeviceIdType.MESH,
        )

    for j in range(SUBS):
        for r in range(RINGS):
            own_copy(r, j).wait()
    pl.semaphore_wait(barrier, 7)
    for j in range(SUBS):
        for r in range(RINGS):
            ring_copy(r, j, 0).start()

    def slot_of(b):
        return slot_ref[block_ref[b]]

    dn_in.wait()
    up_in.wait()
    slot_copy.wait()
    block_copy.wait()

    def stage(q, carry):
        pick = 0
        for i in range(blocks_here):
            slot = slot_of(q * blocks_here + i)
            pick = jnp.where(slot // stored == g, slot % stored, pick)
        dn_st[q] = dn_v[pick]
        up_st[q] = up_v[pick]
        return carry

    def tell(i):
        if i == 2:
            signal(ready.at[2], {"grp": other})
        else:
            for d in (CORES << i, groups - (CORES << i)):
                signal(ready.at[i], {"grp": (g + d) % groups})

    def hear(i):
        pl.semaphore_wait(ready.at[i], 1 if i == 2 else 2)

    tell(0)
    lax.fori_loop(0, groups, stage, 0)
    dn_rc[g] = dn_st[g]
    up_rc[g] = up_st[g]

    def panel_copy(st, rc, send, recv, d):
        q = (g + d) % groups
        return pltpu.make_async_remote_copy(
            src_ref=st.at[q],
            dst_ref=rc.at[g],
            send_sem=send.at[d],
            recv_sem=recv.at[d],
            device_id={"grp": q},
            device_id_type=pl.DeviceIdType.MESH,
        )

    def panel_arrival(st, rc, send, recv, d):
        q = (g + groups - d) % groups
        return pltpu.make_async_remote_copy(
            src_ref=st.at[q],
            dst_ref=rc.at[q],
            send_sem=send.at[d],
            recv_sem=recv.at[d],
            device_id={"grp": q},
            device_id_type=pl.DeviceIdType.MESH,
        )

    acc[...] = jnp.zeros_like(acc)

    def part_value(q, ring, sub, s):
        owner = slot_of(g * blocks_here + q // per_block) // stored
        panel = dn_rc[owner]
        twice = jnp.concatenate([panel, panel], axis=0)
        p = lax.dot_general(
            gat[ring, sub, s], twice, (((1,), (1,)), ((), ())), preferred_element_type=jnp.float32
        )
        lane = lax.broadcasted_iota(jnp.int32, (rows // 2, p.shape[1]), 1)
        return jnp.where(lane < p.shape[1] // 2, p[: rows // 2], p[rows // 2 :])

    def part_copy(d):
        return pltpu.make_async_remote_copy(
            src_ref=part_st.at[d],
            dst_ref=part_rc.at[m],
            send_sem=part_send.at[d],
            recv_sem=part_recv.at[m],
            device_id={"tp": (m + d) % members},
            device_id_type=pl.DeviceIdType.MESH,
        )

    def part_arrival(d):
        q = (m + d) % members
        return pltpu.make_async_remote_copy(
            src_ref=part_st.at[0],
            dst_ref=part_rc.at[q],
            send_sem=part_send.at[0],
            recv_sem=part_recv.at[q],
            device_id={"tp": q},
            device_id_type=pl.DeviceIdType.MESH,
        )

    def my_part(d):
        q = (m + d) % members
        ring, sub = carrier(q, m)
        turned, step = ring // 2, 1 - 2 * (ring % 2)
        s = (step * (ring_time(x, y, turned) - ring_time(q // SIDE, q % SIDE, turned)) + members) % members
        return part_value(q, ring, sub, s)

    def send_part(d):
        part_st[d] = my_part(d)
        part_copy(d).start()

    def add(r, s, value):
        at = pl.multiple_of(source(r, s) * rows, rows)
        acc[pl.ds(at, rows), :] += value

    def product(r, j, s):
        w = w_v[feature(source(r, s), r, j)]
        return jnp.dot(gat[r, j, s], w, preferred_element_type=jnp.float32)

    def multiply(r, s):
        total = product(r, 0, s)
        for j in range(1, SUBS):
            total += product(r, j, s)
        add(r, s, total)

    def phase(j, s, forward=True):
        for r in range(RINGS):
            ring_arrival(r, j, s).wait_recv()
            if forward:
                ring_copy(r, j, s).start()
        for r in range(RINGS):
            add(r, s, product(r, j, s))

    def plain_step(s, carry):
        def sub(j, c):
            phase(j, s)
            return c

        lax.fori_loop(0, SUBS, sub, 0)
        return carry

    def part_step(s, carry):
        def sub(j, c):
            phase(j, s)
            for i in range(2):
                d = 1 + 2 * SUBS * (s - EARLY - 1) + 2 * j + i

                @pl.when(d < members)
                def _():
                    send_part(d)

            return c

        lax.fori_loop(0, SUBS, sub, 0)
        return carry

    for c in range(CHUNKS):
        w_copy(c).wait()
    phase(0, 1)
    multiply(0, 0)
    phase(1, 1)
    hear(0)
    tell(1)
    phase(2, 1)
    multiply(1, 0)
    phase(3, 1)
    hear(1)
    tell(2)
    phase(0, 2)
    multiply(2, 0)
    phase(1, 2)
    hear(2)
    for d in range(1, groups):
        panel_copy(dn_st, dn_rc, dn_send, dn_recv, d).start()
    phase(2, 2)
    for d in range(1, groups):
        panel_copy(up_st, up_rc, up_send, up_recv, d).start()
    phase(3, 2)
    multiply(3, 0)
    lax.fori_loop(3, EARLY + 1, plain_step, 0)
    for d in range(1, groups):
        panel_arrival(dn_st, dn_rc, dn_send, dn_recv, d).wait_recv()
    part_rc[m] = my_part(0)
    lax.fori_loop(EARLY + 1, EARLY + 3, part_step, 0)
    lax.fori_loop(EARLY + 3, EARLY + 5, plain_step, 0)

    def sh_copy(d):
        return pltpu.make_async_remote_copy(
            src_ref=sh_st,
            dst_ref=sh_all.at[m],
            send_sem=sh_send.at[d],
            recv_sem=sh_recv.at[d],
            device_id={"tp": (m + d) % members},
            device_id_type=pl.DeviceIdType.MESH,
        )

    def sh_arrival(d):
        q = (m + members - d) % members
        return pltpu.make_async_remote_copy(
            src_ref=sh_st,
            dst_ref=sh_all.at[q],
            send_sem=sh_send.at[d],
            recv_sem=sh_recv.at[d],
            device_id={"tp": q},
            device_id_type=pl.DeviceIdType.MESH,
        )

    for d in range(1, members):
        part_arrival(d).wait_recv()
    total = part_rc[0]
    for i in range(1, members):
        total += part_rc[i]
    shrink = total.astype(jnp.bfloat16)
    sh_st[...] = shrink
    sh_all[m] = shrink
    for d in range(1, members):
        sh_copy(d).start()
    lax.fori_loop(EARLY + 5, members - 2, plain_step, 0)

    def update(b):
        owner = slot_of(g * blocks_here + b) // stored
        packed = [sh_all[per_block * b + i].astype(jnp.float32) for i in range(per_block)]
        lane = lax.broadcasted_iota(jnp.int32, packed[0].shape, 1)
        low = lane < packed[0].shape[1] // 2
        split = [jnp.where(low == first, p, 0.0) for p in packed for first in (True, False)]
        s = jnp.concatenate(split, axis=0).astype(jnp.bfloat16)
        panel = up_rc[owner]
        twice = jnp.concatenate([panel, panel], axis=0)
        value = jnp.dot(s, twice, preferred_element_type=jnp.float32)
        at = pl.multiple_of(b * BLOCK, BLOCK)
        acc[pl.ds(at, BLOCK), :] += SCALE * value

    def before_last(j, carry):
        phase(j, members - 2)
        return carry

    def before_last_update(j, carry):
        phase(j, members - 2)
        share = blocks_here // (SUBS // 2)
        lax.fori_loop(0, share, lambda i, c: (update(share * (j - SUBS // 2) + i), c)[1], 0)
        return carry

    lax.fori_loop(0, SUBS // 2, before_last, 0)
    for d in range(1, groups):
        panel_arrival(up_st, up_rc, up_send, up_recv, d).wait_recv()
    for d in range(1, members):
        sh_arrival(d).wait_recv()
    lax.fori_loop(SUBS // 2, SUBS, before_last_update, 0)

    def last(j, carry):
        phase(j, members - 1, forward=False)
        return carry

    lax.fori_loop(0, SUBS, last, 0)

    def finish(b, carry):
        at = pl.multiple_of(b * BLOCK, BLOCK)
        out_ref[pl.ds(at, BLOCK), :] = acc[pl.ds(at, BLOCK), :].astype(out_ref.dtype)
        return carry

    lax.fori_loop(0, blocks_here, finish, 0)

    for r in range(RINGS):
        whole = gat.at[r, :, pl.ds(0, members - 1)]
        pltpu.make_async_remote_copy(
            src_ref=whole,
            dst_ref=whole,
            send_sem=ring_send.at[r],
            recv_sem=ring_recv.at[r, 0, 0],
            device_id={"tp": nexts[r]},
            device_id_type=pl.DeviceIdType.MESH,
        ).wait_send()
    for d in range(1, groups):
        panel_copy(dn_st, dn_rc, dn_send, dn_recv, d).wait_send()
        panel_copy(up_st, up_rc, up_send, up_recv, d).wait_send()
    for s in range(1, members):
        part_copy(s).wait_send()
        sh_copy(s).wait_send()


def local(tokens, frozen_weight, down_weight, up_weight, adapter_storage_slot, adapter_of_block):
    groups = lax.axis_size("grp")
    members = lax.axis_size("tp")
    rows, width = tokens.shape
    rank, down_width = down_weight.shape[1:]
    columns = frozen_weight.shape[1]
    chunk = width // (RINGS * SUBS)
    bf16, f32 = jnp.bfloat16, jnp.float32
    hbm_spec = pl.BlockSpec(memory_space=pltpu.HBM)
    dma = pltpu.SemaphoreType.DMA
    return pl.pallas_call(
        kernel,
        out_shape=jax.ShapeDtypeStruct((members * rows, columns), bf16),
        in_specs=[hbm_spec, hbm_spec, hbm_spec, hbm_spec, hbm_spec, hbm_spec],
        out_specs=pl.BlockSpec(memory_space=pltpu.VMEM),
        scratch_shapes=[
            pltpu.SMEM(adapter_storage_slot.shape, jnp.int32),
            pltpu.SMEM(adapter_of_block.shape, jnp.int32),
            pltpu.VMEM((RINGS, SUBS, members, rows, chunk), bf16),
            pltpu.VMEM((CHUNKS, chunk, columns), bf16),
            pltpu.VMEM(down_weight.shape, bf16),
            pltpu.VMEM(up_weight.shape, bf16),
            pltpu.VMEM((groups, rank, down_width), bf16),
            pltpu.VMEM((groups, rank, columns), bf16),
            pltpu.VMEM((groups, rank, down_width), bf16),
            pltpu.VMEM((groups, rank, columns), bf16),
            pltpu.VMEM((members * rows, columns), f32),
            pltpu.VMEM((members, rows // 2, 2 * rank), f32),
            pltpu.VMEM((members, rows // 2, 2 * rank), f32),
            pltpu.VMEM((rows // 2, 2 * rank), bf16),
            pltpu.VMEM((members, rows // 2, 2 * rank), bf16),
            dma((RINGS, SUBS)),
            dma((CHUNKS,)),
            dma((4,)),
            dma((RINGS,)),
            dma((RINGS, SUBS, members)),
            dma((groups,)),
            dma((groups,)),
            dma((groups,)),
            dma((groups,)),
            dma((members,)),
            dma((members,)),
            dma((members,)),
            dma((members,)),
            pltpu.SemaphoreType.REGULAR((3,)),
        ],
        compiler_params=pltpu.CompilerParams(
            collective_id=0, has_side_effects=True, vmem_limit_bytes=42 << 20
        ),
        cost_estimate=pl.CostEstimate(
            flops=2 * members * rows * width * columns,
            bytes_accessed=2 * width * columns + 2 * members * rows * columns,
            transcendentals=0,
        ),
        name="projection",
    )(
        *[
            pltpu.with_memory_space_constraint(a, pltpu.HBM)
            for a in (adapter_storage_slot, adapter_of_block, tokens, frozen_weight, down_weight, up_weight)
        ]
    )


def solution(mesh):
    placed = (
        P(("grp", "tp"), None),
        P(None, "tp"),
        P("grp", None, "tp"),
        P("grp", None, "tp"),
        P(),
        P(),
    )
    return jax.shard_map(
        local, mesh=mesh, in_specs=placed, out_specs=P("grp", "tp"), check_vma=False
    )
```

```python
import jax
import jax.numpy as jnp
from jax import lax
from jax.experimental import pallas as pl
from jax.experimental.pallas import tpu as pltpu
from jax.sharding import PartitionSpec as P

BLOCK = 128
CORES = 2
SIDE = 4
RINGS = 4
SUBS = 4
SCALE = 0.5
CHUNKS = RINGS * SUBS
EARLY = 8


def ring_time(x, y, turned):
    major = (1 - turned) * x + turned * y
    return SIDE * major + (x + y) % SIDE


def ring_node(t, turned):
    major = t // SIDE
    minor = (t % SIDE + SIDE - major) % SIDE
    return (1 - turned) * (SIDE * major + minor) + turned * (SIDE * minor + major)


RIDES = ((378, 53229, 18521, 15202), (6059, 53229, 22822, 33795), (10155, 53229, 25348, 38168), (15032, 53229, 1045, 30249))
CARRIERS = ((64547, 7579, 57482, 25927), (51517, 10430, 431, 25927), (41945, 11240, 508, 25927), (15771, 65162, 4800, 25927))


def pick(table, index):
    value = table[0]
    for i in range(1, len(table)):
        value = jnp.where(index == i, table[i], value)
    return value


def feature(member, r, j):
    x, y = member // SIDE, member % SIDE
    k = lax.shift_right_logical(pick([row[r] for row in RIDES], (x + y) % SIDE), 4 * j) % CHUNKS
    return SIDE * ((k // SIDE + x) % SIDE) + (k % SIDE + SIDE - x) % SIDE


def carrier(member, chunk):
    x, y = member // SIDE, member % SIDE
    i, k = (chunk // SIDE + SIDE - x) % SIDE, (chunk % SIDE + x) % SIDE
    entry = pick([pick(row, i) for row in CARRIERS], (x + y) % SIDE)
    at = lax.shift_right_logical(entry, 4 * k) % CHUNKS
    return at // SUBS, at % SUBS


def kernel(
    slot_in, block_in, tokens_ref, weight_ref, down_ref, up_ref, out_ref,
    slot_ref, block_ref, gat, w_v, dn_v, up_v, dn_st, up_st, dn_rc, up_rc, acc, part_out, part_in, part_st, part_rc, sh_st, sh_all,
    own_sem, w_sem, ad_sem, ring_send, ring_recv, dn_send, dn_recv, up_send, up_recv,
    pair_sem, part_send, part_recv, sh_send, sh_recv, ready,
):
    groups = lax.axis_size("grp")
    members = lax.axis_size("tp")
    g = lax.axis_index("grp")
    m = lax.axis_index("tp")
    x, y = m // SIDE, m % SIDE
    rows = tokens_ref.shape[0]
    chunk = gat.shape[4]
    stored = down_ref.shape[0]
    blocks_here = members * rows // BLOCK
    per_block = BLOCK // rows

    def signal(sem, where):
        pl.semaphore_signal(sem, inc=1, device_id=where, device_id_type=pl.DeviceIdType.MESH)

    other = g + 1 - 2 * (g % CORES)
    barrier = pltpu.get_barrier_semaphore()
    for d in (1, SIDE - 1):
        signal(barrier, {"tp": SIDE * ((x + d) % SIDE) + y})
        signal(barrier, {"tp": SIDE * x + (y + d) % SIDE})
    for d in (CORES, groups - CORES):
        signal(barrier, {"grp": (g + d) % groups})
    signal(barrier, {"grp": other})

    def own_copy(r, j):
        start = pl.multiple_of(feature(m, r, j) * chunk, chunk)
        return pltpu.make_async_copy(
            tokens_ref.at[:, pl.ds(start, chunk)], gat.at[r, j, 0], own_sem.at[r, j]
        )

    def w_copy(c):
        return pltpu.make_async_copy(weight_ref.at[pl.ds(c * chunk, chunk), :], w_v.at[c], w_sem.at[c])

    for r in range(RINGS):
        for j in range(SUBS):
            own_copy(r, j).start()
    dn_in = pltpu.make_async_copy(down_ref, dn_v, ad_sem.at[0])
    up_in = pltpu.make_async_copy(up_ref, up_v, ad_sem.at[1])
    slot_copy = pltpu.make_async_copy(slot_in, slot_ref, ad_sem.at[2])
    block_copy = pltpu.make_async_copy(block_in, block_ref, ad_sem.at[3])
    dn_in.start()
    up_in.start()
    slot_copy.start()
    block_copy.start()
    for c in range(CHUNKS):
        w_copy(c).start()

    times = [ring_time(x, y, r // 2) for r in range(RINGS)]

    def source(r, s):
        step = 1 - 2 * (r % 2)
        return ring_node((times[r] - step * s + members) % members, r // 2)

    nexts = [
        ring_node((times[r] + 1 - 2 * (r % 2) + members) % members, r // 2) for r in range(RINGS)
    ]

    def ring_copy(r, j, s):
        return pltpu.make_async_remote_copy(
            src_ref=gat.at[r, j, s],
            dst_ref=gat.at[r, j, s + 1],
            send_sem=ring_send.at[r],
            recv_sem=ring_recv.at[r, j, s + 1],
            device_id={"tp": nexts[r]},
            device_id_type=pl.DeviceIdType.MESH,
        )

    def ring_arrival(r, j, s):
        return pltpu.make_async_remote_copy(
            src_ref=gat.at[r, j, s],
            dst_ref=gat.at[r, j, s],
            send_sem=ring_send.at[r],
            recv_sem=ring_recv.at[r, j, s],
            device_id={"tp": nexts[r]},
            device_id_type=pl.DeviceIdType.MESH,
        )

    for j in range(SUBS):
        for r in range(RINGS):
            own_copy(r, j).wait()
    pl.semaphore_wait(barrier, 7)
    for j in range(SUBS):
        for r in range(RINGS):
            ring_copy(r, j, 0).start()

    def slot_of(b):
        return slot_ref[block_ref[b]]

    dn_in.wait()
    up_in.wait()
    slot_copy.wait()
    block_copy.wait()

    def stage(q, carry):
        pick = 0
        for i in range(blocks_here):
            slot = slot_of(q * blocks_here + i)
            pick = jnp.where(slot // stored == g, slot % stored, pick)
        dn_st[q] = dn_v[pick]
        up_st[q] = up_v[pick]
        return carry

    def tell(i):
        if i == 2:
            signal(ready.at[2], {"grp": other})
        else:
            for d in (CORES << i, groups - (CORES << i)):
                signal(ready.at[i], {"grp": (g + d) % groups})

    def hear(i):
        pl.semaphore_wait(ready.at[i], 1 if i == 2 else 2)

    tell(0)
    lax.fori_loop(0, groups, stage, 0)
    dn_rc[g] = dn_st[g]
    up_rc[g] = up_st[g]

    def panel_copy(st, rc, send, recv, d):
        q = (g + d) % groups
        return pltpu.make_async_remote_copy(
            src_ref=st.at[q],
            dst_ref=rc.at[g],
            send_sem=send.at[d],
            recv_sem=recv.at[d],
            device_id={"grp": q},
            device_id_type=pl.DeviceIdType.MESH,
        )

    def panel_arrival(st, rc, send, recv, d):
        q = (g + groups - d) % groups
        return pltpu.make_async_remote_copy(
            src_ref=st.at[q],
            dst_ref=rc.at[q],
            send_sem=send.at[d],
            recv_sem=recv.at[d],
            device_id={"grp": q},
            device_id_type=pl.DeviceIdType.MESH,
        )

    acc[...] = jnp.zeros_like(acc)

    def part_value(q, ring, sub, s):
        owner = slot_of(g * blocks_here + q // per_block) // stored
        panel = dn_rc[owner]
        twice = jnp.concatenate([panel, panel], axis=0)
        p = lax.dot_general(
            gat[ring, sub, s], twice, (((1,), (1,)), ((), ())), preferred_element_type=jnp.float32
        )
        lane = lax.broadcasted_iota(jnp.int32, (rows // 2, p.shape[1]), 1)
        return jnp.where(lane < p.shape[1] // 2, p[: rows // 2], p[rows // 2 :])

    side = ((y + 1) // 2) % 2
    partner = m + 1 - 2 * (y % 2)
    shared = members // 2

    def homes(kind, i):
        return SIDE * (i // 2) + kind * (1 + i % 2) + (1 - kind) * 3 * (i % 2)

    def pair_copy():
        return pltpu.make_async_remote_copy(
            src_ref=part_out,
            dst_ref=part_in,
            send_sem=pair_sem.at[0],
            recv_sem=pair_sem.at[1],
            device_id={"tp": partner},
            device_id_type=pl.DeviceIdType.MESH,
        )

    def part_copy(i):
        return pltpu.make_async_remote_copy(
            src_ref=part_st.at[i],
            dst_ref=part_rc.at[m],
            send_sem=part_send.at[i],
            recv_sem=part_recv.at[m],
            device_id={"tp": homes(side, i)},
            device_id_type=pl.DeviceIdType.MESH,
        )

    def part_arrival(q):
        return pltpu.make_async_remote_copy(
            src_ref=part_st.at[0],
            dst_ref=part_rc.at[q],
            send_sem=part_send.at[0],
            recv_sem=part_recv.at[q],
            device_id={"tp": q},
            device_id_type=pl.DeviceIdType.MESH,
        )

    def my_part(q):
        ring, sub = carrier(q, m)
        turned, step = ring // 2, 1 - 2 * (ring % 2)
        s = (step * (ring_time(x, y, turned) - ring_time(q // SIDE, q % SIDE, turned)) + members) % members
        return part_value(q, ring, sub, s)

    def add(r, s, value):
        at = pl.multiple_of(source(r, s) * rows, rows)
        acc[pl.ds(at, rows), :] += value

    def product(r, j, s):
        w = w_v[feature(source(r, s), r, j)]
        return jnp.dot(gat[r, j, s], w, preferred_element_type=jnp.float32)

    def multiply(r, s):
        total = product(r, 0, s)
        for j in range(1, SUBS):
            total += product(r, j, s)
        add(r, s, total)

    def phase(j, s, forward=True):
        for r in range(RINGS):
            ring_arrival(r, j, s).wait_recv()
            if forward:
                ring_copy(r, j, s).start()
        for r in range(RINGS):
            add(r, s, product(r, j, s))

    def plain_step(s, carry):
        def sub(j, c):
            phase(j, s)
            return c

        lax.fori_loop(0, SUBS, sub, 0)
        return carry

    def part_step(s, kind, into):
        def sub(j, c):
            phase(j, s)
            for i in range(shared // SUBS):
                at = shared // SUBS * j + i
                into[at] = my_part(homes(kind, at))
            return c

        lax.fori_loop(0, SUBS, sub, 0)

    for c in range(CHUNKS):
        w_copy(c).wait()
    phase(0, 1)
    multiply(0, 0)
    phase(1, 1)
    hear(0)
    tell(1)
    phase(2, 1)
    multiply(1, 0)
    phase(3, 1)
    hear(1)
    tell(2)
    phase(0, 2)
    multiply(2, 0)
    phase(1, 2)
    hear(2)
    for d in range(1, groups):
        panel_copy(dn_st, dn_rc, dn_send, dn_recv, d).start()
    phase(2, 2)
    for d in range(1, groups):
        panel_copy(up_st, up_rc, up_send, up_recv, d).start()
    phase(3, 2)
    multiply(3, 0)
    lax.fori_loop(3, EARLY + 1, plain_step, 0)
    for d in range(1, groups):
        panel_arrival(dn_st, dn_rc, dn_send, dn_recv, d).wait_recv()
    part_step(EARLY + 1, 1 - side, part_out)
    pair_copy().start()
    part_step(EARLY + 2, side, part_st)
    pair_copy().wait_recv()
    part_st[...] += part_in[...]
    for i in range(shared):

        @pl.when(homes(side, i) == m)
        def _():
            part_rc[m] = part_st[i]

        @pl.when(homes(side, i) != m)
        def _():
            part_copy(i).start()

    lax.fori_loop(EARLY + 3, EARLY + 5, plain_step, 0)

    def sh_copy(d):
        return pltpu.make_async_remote_copy(
            src_ref=sh_st,
            dst_ref=sh_all.at[m],
            send_sem=sh_send.at[d],
            recv_sem=sh_recv.at[d],
            device_id={"tp": (m + d) % members},
            device_id_type=pl.DeviceIdType.MESH,
        )

    def sh_arrival(d):
        q = (m + members - d) % members
        return pltpu.make_async_remote_copy(
            src_ref=sh_st,
            dst_ref=sh_all.at[q],
            send_sem=sh_send.at[d],
            recv_sem=sh_recv.at[d],
            device_id={"tp": q},
            device_id_type=pl.DeviceIdType.MESH,
        )

    for i in range(shared):

        @pl.when(homes(side, i) != m)
        def _():
            part_arrival(homes(side, i)).wait_recv()

    total = part_rc[homes(side, 0)]
    for i in range(1, shared):
        total += part_rc[homes(side, i)]
    shrink = total.astype(jnp.bfloat16)
    sh_st[...] = shrink
    sh_all[m] = shrink
    for d in range(1, members):
        sh_copy(d).start()
    lax.fori_loop(EARLY + 5, members - 2, plain_step, 0)

    def update(b):
        owner = slot_of(g * blocks_here + b) // stored
        packed = [sh_all[per_block * b + i].astype(jnp.float32) for i in range(per_block)]
        lane = lax.broadcasted_iota(jnp.int32, packed[0].shape, 1)
        low = lane < packed[0].shape[1] // 2
        split = [jnp.where(low == first, p, 0.0) for p in packed for first in (True, False)]
        s = jnp.concatenate(split, axis=0).astype(jnp.bfloat16)
        panel = up_rc[owner]
        twice = jnp.concatenate([panel, panel], axis=0)
        value = jnp.dot(s, twice, preferred_element_type=jnp.float32)
        at = pl.multiple_of(b * BLOCK, BLOCK)
        acc[pl.ds(at, BLOCK), :] += SCALE * value

    def before_last(j, carry):
        phase(j, members - 2)
        return carry

    def before_last_update(j, carry):
        phase(j, members - 2)
        share = blocks_here // (SUBS // 2)
        lax.fori_loop(0, share, lambda i, c: (update(share * (j - SUBS // 2) + i), c)[1], 0)
        return carry

    lax.fori_loop(0, SUBS // 2, before_last, 0)
    for d in range(1, groups):
        panel_arrival(up_st, up_rc, up_send, up_recv, d).wait_recv()
    for d in range(1, members):
        sh_arrival(d).wait_recv()
    for d in range(1, groups):
        panel_copy(dn_st, dn_rc, dn_send, dn_recv, d).wait_send()
        panel_copy(up_st, up_rc, up_send, up_recv, d).wait_send()
    pair_copy().wait_send()
    for i in range(shared):

        @pl.when(homes(side, i) != m)
        def _():
            part_copy(i).wait_send()

    for d in range(1, members):
        sh_copy(d).wait_send()
    lax.fori_loop(SUBS // 2, SUBS, before_last_update, 0)

    def last(j, carry):
        phase(j, members - 1, forward=False)
        return carry

    lax.fori_loop(0, SUBS, last, 0)

    def finish(b, carry):
        at = pl.multiple_of(b * BLOCK, BLOCK)
        out_ref[pl.ds(at, BLOCK), :] = acc[pl.ds(at, BLOCK), :].astype(out_ref.dtype)
        return carry

    lax.fori_loop(0, blocks_here, finish, 0)

    for r in range(RINGS):
        whole = gat.at[r, :, pl.ds(0, members - 1)]
        pltpu.make_async_remote_copy(
            src_ref=whole,
            dst_ref=whole,
            send_sem=ring_send.at[r],
            recv_sem=ring_recv.at[r, 0, 0],
            device_id={"tp": nexts[r]},
            device_id_type=pl.DeviceIdType.MESH,
        ).wait_send()


def local(tokens, frozen_weight, down_weight, up_weight, adapter_storage_slot, adapter_of_block):
    groups = lax.axis_size("grp")
    members = lax.axis_size("tp")
    rows, width = tokens.shape
    rank, down_width = down_weight.shape[1:]
    columns = frozen_weight.shape[1]
    chunk = width // (RINGS * SUBS)
    bf16, f32 = jnp.bfloat16, jnp.float32
    hbm_spec = pl.BlockSpec(memory_space=pltpu.HBM)
    dma = pltpu.SemaphoreType.DMA
    return pl.pallas_call(
        kernel,
        out_shape=jax.ShapeDtypeStruct((members * rows, columns), bf16),
        in_specs=[hbm_spec, hbm_spec, hbm_spec, hbm_spec, hbm_spec, hbm_spec],
        out_specs=pl.BlockSpec(memory_space=pltpu.VMEM),
        scratch_shapes=[
            pltpu.SMEM(adapter_storage_slot.shape, jnp.int32),
            pltpu.SMEM(adapter_of_block.shape, jnp.int32),
            pltpu.VMEM((RINGS, SUBS, members, rows, chunk), bf16),
            pltpu.VMEM((CHUNKS, chunk, columns), bf16),
            pltpu.VMEM(down_weight.shape, bf16),
            pltpu.VMEM(up_weight.shape, bf16),
            pltpu.VMEM((groups, rank, down_width), bf16),
            pltpu.VMEM((groups, rank, columns), bf16),
            pltpu.VMEM((groups, rank, down_width), bf16),
            pltpu.VMEM((groups, rank, columns), bf16),
            pltpu.VMEM((members * rows, columns), f32),
            pltpu.VMEM((members // 2, rows // 2, 2 * rank), f32),
            pltpu.VMEM((members // 2, rows // 2, 2 * rank), f32),
            pltpu.VMEM((members // 2, rows // 2, 2 * rank), f32),
            pltpu.VMEM((members, rows // 2, 2 * rank), f32),
            pltpu.VMEM((rows // 2, 2 * rank), bf16),
            pltpu.VMEM((members, rows // 2, 2 * rank), bf16),
            dma((RINGS, SUBS)),
            dma((CHUNKS,)),
            dma((4,)),
            dma((RINGS,)),
            dma((RINGS, SUBS, members)),
            dma((groups,)),
            dma((groups,)),
            dma((groups,)),
            dma((groups,)),
            dma((2,)),
            dma((members,)),
            dma((members,)),
            dma((members,)),
            dma((members,)),
            pltpu.SemaphoreType.REGULAR((3,)),
        ],
        compiler_params=pltpu.CompilerParams(
            collective_id=0, has_side_effects=True, vmem_limit_bytes=42 << 20
        ),
        cost_estimate=pl.CostEstimate(
            flops=2 * members * rows * width * columns,
            bytes_accessed=2 * width * columns + 2 * members * rows * columns,
            transcendentals=0,
        ),
        name="projection",
    )(
        *[
            pltpu.with_memory_space_constraint(a, pltpu.HBM)
            for a in (adapter_storage_slot, adapter_of_block, tokens, frozen_weight, down_weight, up_weight)
        ]
    )


def solution(mesh):
    placed = (
        P(("grp", "tp"), None),
        P(None, "tp"),
        P("grp", None, "tp"),
        P("grp", None, "tp"),
        P(),
        P(),
    )
    return jax.shard_map(
        local, mesh=mesh, in_specs=placed, out_specs=P("grp", "tp"), check_vma=False
    )
```

```python
import jax
import jax.numpy as jnp
from jax import lax
from jax.experimental import pallas as pl
from jax.experimental.pallas import tpu as pltpu
from jax.sharding import PartitionSpec as P

BLOCK = 128
CORES = 2
SIDE = 4
RINGS = 4
SUBS = 4
SCALE = 0.5
CHUNKS = RINGS * SUBS
EARLY = 8


def ring_time(x, y, turned):
    major = (1 - turned) * x + turned * y
    return SIDE * major + (x + y) % SIDE


def ring_node(t, turned):
    major = t // SIDE
    minor = (t % SIDE + SIDE - major) % SIDE
    return (1 - turned) * (SIDE * major + minor) + turned * (SIDE * minor + major)


RIDES = ((378, 53229, 18521, 15202), (6059, 53229, 22822, 33795), (10155, 53229, 25348, 38168), (15032, 53229, 1045, 30249))
CARRIERS = ((64547, 7579, 57482, 25927), (51517, 10430, 431, 25927), (41945, 11240, 508, 25927), (15771, 65162, 4800, 25927))


def pick(table, index):
    value = table[0]
    for i in range(1, len(table)):
        value = jnp.where(index == i, table[i], value)
    return value


def feature(member, r, j):
    x, y = member // SIDE, member % SIDE
    k = lax.shift_right_logical(pick([row[r] for row in RIDES], (x + y) % SIDE), 4 * j) % CHUNKS
    return SIDE * ((k // SIDE + x) % SIDE) + (k % SIDE + SIDE - x) % SIDE


def carrier(member, chunk):
    x, y = member // SIDE, member % SIDE
    i, k = (chunk // SIDE + SIDE - x) % SIDE, (chunk % SIDE + x) % SIDE
    entry = pick([pick(row, i) for row in CARRIERS], (x + y) % SIDE)
    at = lax.shift_right_logical(entry, 4 * k) % CHUNKS
    return at // SUBS, at % SUBS


def kernel(
    slot_in, block_in, tokens_ref, weight_ref, down_ref, up_ref, out_ref,
    slot_ref, block_ref, gat, w_v, dn_v, up_v, dn_st, up_st, dn_rc, up_rc, acc, part_out, part_in, part_st, part_rc, sh_st, sh_all,
    own_sem, w_sem, ad_sem, ring_send, ring_recv, dn_send, dn_recv, up_send, up_recv,
    pair_sem, part_send, part_recv, sh_send, sh_recv, ready,
):
    groups = lax.axis_size("grp")
    members = lax.axis_size("tp")
    g = lax.axis_index("grp")
    m = lax.axis_index("tp")
    x, y = m // SIDE, m % SIDE
    rows = tokens_ref.shape[0]
    chunk = gat.shape[4]
    stored = down_ref.shape[0]
    blocks_here = members * rows // BLOCK
    per_block = BLOCK // rows

    def signal(sem, where):
        pl.semaphore_signal(sem, inc=1, device_id=where, device_id_type=pl.DeviceIdType.MESH)

    other = g + 1 - 2 * (g % CORES)
    barrier = pltpu.get_barrier_semaphore()
    for d in (1, SIDE - 1):
        signal(barrier, {"tp": SIDE * ((x + d) % SIDE) + y})
        signal(barrier, {"tp": SIDE * x + (y + d) % SIDE})
    for d in (CORES, groups - CORES):
        signal(barrier, {"grp": (g + d) % groups})
    signal(barrier, {"grp": other})

    def own_copy(r, j):
        start = pl.multiple_of(feature(m, r, j) * chunk, chunk)
        return pltpu.make_async_copy(
            tokens_ref.at[:, pl.ds(start, chunk)], gat.at[r, j, 0], own_sem.at[r, j]
        )

    def w_copy(c):
        return pltpu.make_async_copy(weight_ref.at[pl.ds(c * chunk, chunk), :], w_v.at[c], w_sem.at[c])

    for r in range(RINGS):
        for j in range(SUBS):
            own_copy(r, j).start()
    dn_in = pltpu.make_async_copy(down_ref, dn_v, ad_sem.at[0])
    up_in = pltpu.make_async_copy(up_ref, up_v, ad_sem.at[1])
    slot_copy = pltpu.make_async_copy(slot_in, slot_ref, ad_sem.at[2])
    block_copy = pltpu.make_async_copy(block_in, block_ref, ad_sem.at[3])
    dn_in.start()
    up_in.start()
    slot_copy.start()
    block_copy.start()
    for c in range(CHUNKS):
        w_copy(c).start()

    times = [ring_time(x, y, r // 2) for r in range(RINGS)]

    def source(r, s):
        step = 1 - 2 * (r % 2)
        return ring_node((times[r] - step * s + members) % members, r // 2)

    nexts = [
        ring_node((times[r] + 1 - 2 * (r % 2) + members) % members, r // 2) for r in range(RINGS)
    ]

    def ring_copy(r, j, s):
        return pltpu.make_async_remote_copy(
            src_ref=gat.at[r, j, s],
            dst_ref=gat.at[r, j, s + 1],
            send_sem=ring_send.at[r],
            recv_sem=ring_recv.at[r, j, s + 1],
            device_id={"tp": nexts[r]},
            device_id_type=pl.DeviceIdType.MESH,
        )

    def ring_arrival(r, j, s):
        return pltpu.make_async_remote_copy(
            src_ref=gat.at[r, j, s],
            dst_ref=gat.at[r, j, s],
            send_sem=ring_send.at[r],
            recv_sem=ring_recv.at[r, j, s],
            device_id={"tp": nexts[r]},
            device_id_type=pl.DeviceIdType.MESH,
        )

    for j in range(SUBS):
        for r in range(RINGS):
            own_copy(r, j).wait()
    pl.semaphore_wait(barrier, 7)
    for j in range(SUBS):
        for r in range(RINGS):
            ring_copy(r, j, 0).start()

    def slot_of(b):
        return slot_ref[block_ref[b]]

    dn_in.wait()
    up_in.wait()
    slot_copy.wait()
    block_copy.wait()

    def stage(q, carry):
        pick = 0
        for i in range(blocks_here):
            slot = slot_of(q * blocks_here + i)
            pick = jnp.where(slot // stored == g, slot % stored, pick)
        dn_st[q] = dn_v[pick]
        up_st[q] = up_v[pick]
        return carry

    def tell(i):
        if i == 2:
            signal(ready.at[2], {"grp": other})
        else:
            for d in (CORES << i, groups - (CORES << i)):
                signal(ready.at[i], {"grp": (g + d) % groups})

    def hear(i):
        pl.semaphore_wait(ready.at[i], 1 if i == 2 else 2)

    tell(0)
    lax.fori_loop(0, groups, stage, 0)
    dn_rc[g] = dn_st[g]
    up_rc[g] = up_st[g]

    def panel_copy(st, rc, send, recv, d):
        q = (g + d) % groups
        return pltpu.make_async_remote_copy(
            src_ref=st.at[q],
            dst_ref=rc.at[g],
            send_sem=send.at[d],
            recv_sem=recv.at[d],
            device_id={"grp": q},
            device_id_type=pl.DeviceIdType.MESH,
        )

    def panel_arrival(st, rc, send, recv, d):
        q = (g + groups - d) % groups
        return pltpu.make_async_remote_copy(
            src_ref=st.at[q],
            dst_ref=rc.at[q],
            send_sem=send.at[d],
            recv_sem=recv.at[d],
            device_id={"grp": q},
            device_id_type=pl.DeviceIdType.MESH,
        )

    acc[...] = jnp.zeros_like(acc)

    def part_value(q, ring, sub, s):
        owner = slot_of(g * blocks_here + q // per_block) // stored
        panel = dn_rc[owner]
        twice = jnp.concatenate([panel, panel], axis=0)
        p = lax.dot_general(
            gat[ring, sub, s], twice, (((1,), (1,)), ((), ())), preferred_element_type=jnp.float32
        )
        lane = lax.broadcasted_iota(jnp.int32, (rows // 2, p.shape[1]), 1)
        return jnp.where(lane < p.shape[1] // 2, p[: rows // 2], p[rows // 2 :])

    side = ((y + 1) // 2) % 2
    partner = m + 1 - 2 * (y % 2)
    shared = members // 2

    def homes(kind, i):
        return SIDE * (i // 2) + kind * (1 + i % 2) + (1 - kind) * 3 * (i % 2)

    def pair_copy():
        return pltpu.make_async_remote_copy(
            src_ref=part_out,
            dst_ref=part_in,
            send_sem=pair_sem.at[0],
            recv_sem=pair_sem.at[1],
            device_id={"tp": partner},
            device_id_type=pl.DeviceIdType.MESH,
        )

    def part_copy(i):
        return pltpu.make_async_remote_copy(
            src_ref=part_st.at[i],
            dst_ref=part_rc.at[m],
            send_sem=part_send.at[i],
            recv_sem=part_recv.at[m],
            device_id={"tp": homes(side, i)},
            device_id_type=pl.DeviceIdType.MESH,
        )

    def part_arrival(q):
        return pltpu.make_async_remote_copy(
            src_ref=part_st.at[0],
            dst_ref=part_rc.at[q],
            send_sem=part_send.at[0],
            recv_sem=part_recv.at[q],
            device_id={"tp": q},
            device_id_type=pl.DeviceIdType.MESH,
        )

    def my_part(q):
        ring, sub = carrier(q, m)
        turned, step = ring // 2, 1 - 2 * (ring % 2)
        s = (step * (ring_time(x, y, turned) - ring_time(q // SIDE, q % SIDE, turned)) + members) % members
        return part_value(q, ring, sub, s)

    def add(r, s, value):
        at = pl.multiple_of(source(r, s) * rows, rows)
        acc[pl.ds(at, rows), :] += value

    def product(r, j, s):
        w = w_v[feature(source(r, s), r, j)]
        return jnp.dot(gat[r, j, s], w, preferred_element_type=jnp.float32)

    def multiply(r, s):
        total = product(r, 0, s)
        for j in range(1, SUBS):
            total += product(r, j, s)
        add(r, s, total)

    def phase(j, s, forward=True):
        for r in range(RINGS):
            ring_arrival(r, j, s).wait_recv()
            if forward:
                ring_copy(r, j, s).start()
        for r in range(RINGS):
            add(r, s, product(r, j, s))

    def plain_step(s, carry):
        def sub(j, c):
            phase(j, s)
            return c

        lax.fori_loop(0, SUBS, sub, 0)
        return carry

    def part_step(s, kind, into):
        def sub(j, c):
            phase(j, s)
            for i in range(shared // SUBS):
                at = shared // SUBS * j + i
                into[at] = my_part(homes(kind, at))
            return c

        lax.fori_loop(0, SUBS, sub, 0)

    for c in range(CHUNKS):
        w_copy(c).wait()
    phase(0, 1)
    multiply(0, 0)
    phase(1, 1)
    phase(2, 1)
    hear(0)
    tell(1)
    multiply(1, 0)
    phase(3, 1)
    phase(0, 2)
    multiply(2, 0)
    phase(1, 2)
    hear(1)
    tell(2)
    phase(2, 2)
    phase(3, 2)
    hear(2)
    for d in range(1, groups):
        panel_copy(dn_st, dn_rc, dn_send, dn_recv, d).start()
    multiply(3, 0)
    for d in range(1, groups):
        panel_copy(up_st, up_rc, up_send, up_recv, d).start()
    lax.fori_loop(3, EARLY + 1, plain_step, 0)
    for d in range(1, groups):
        panel_arrival(dn_st, dn_rc, dn_send, dn_recv, d).wait_recv()
    part_step(EARLY + 1, 1 - side, part_out)
    pair_copy().start()
    part_step(EARLY + 2, side, part_st)
    pair_copy().wait_recv()
    part_st[...] += part_in[...]
    for i in range(shared):

        @pl.when(homes(side, i) == m)
        def _():
            part_rc[m] = part_st[i]

        @pl.when(homes(side, i) != m)
        def _():
            part_copy(i).start()

    lax.fori_loop(EARLY + 3, EARLY + 5, plain_step, 0)

    def sh_copy(d):
        return pltpu.make_async_remote_copy(
            src_ref=sh_st,
            dst_ref=sh_all.at[m],
            send_sem=sh_send.at[d],
            recv_sem=sh_recv.at[d],
            device_id={"tp": (m + d) % members},
            device_id_type=pl.DeviceIdType.MESH,
        )

    def sh_arrival(d):
        q = (m + members - d) % members
        return pltpu.make_async_remote_copy(
            src_ref=sh_st,
            dst_ref=sh_all.at[q],
            send_sem=sh_send.at[d],
            recv_sem=sh_recv.at[d],
            device_id={"tp": q},
            device_id_type=pl.DeviceIdType.MESH,
        )

    for i in range(shared):

        @pl.when(homes(side, i) != m)
        def _():
            part_arrival(homes(side, i)).wait_recv()

    total = part_rc[homes(side, 0)]
    for i in range(1, shared):
        total += part_rc[homes(side, i)]
    shrink = total.astype(jnp.bfloat16)
    sh_st[...] = shrink
    sh_all[m] = shrink
    for d in range(1, members):
        sh_copy(d).start()
    lax.fori_loop(EARLY + 5, members - 2, plain_step, 0)

    def update(b):
        owner = slot_of(g * blocks_here + b) // stored
        packed = [sh_all[per_block * b + i].astype(jnp.float32) for i in range(per_block)]
        lane = lax.broadcasted_iota(jnp.int32, packed[0].shape, 1)
        low = lane < packed[0].shape[1] // 2
        split = [jnp.where(low == first, p, 0.0) for p in packed for first in (True, False)]
        s = jnp.concatenate(split, axis=0).astype(jnp.bfloat16)
        panel = up_rc[owner]
        twice = jnp.concatenate([panel, panel], axis=0)
        value = jnp.dot(s, twice, preferred_element_type=jnp.float32)
        at = pl.multiple_of(b * BLOCK, BLOCK)
        acc[pl.ds(at, BLOCK), :] += SCALE * value

    def before_last(j, carry):
        phase(j, members - 2)
        return carry

    def before_last_update(j, carry):
        phase(j, members - 2)
        share = blocks_here // (SUBS // 2)
        lax.fori_loop(0, share, lambda i, c: (update(share * (j - SUBS // 2) + i), c)[1], 0)
        return carry

    lax.fori_loop(0, SUBS // 2, before_last, 0)
    for d in range(1, groups):
        panel_arrival(up_st, up_rc, up_send, up_recv, d).wait_recv()
    for d in range(1, members):
        sh_arrival(d).wait_recv()
    for d in range(1, groups):
        panel_copy(dn_st, dn_rc, dn_send, dn_recv, d).wait_send()
        panel_copy(up_st, up_rc, up_send, up_recv, d).wait_send()
    pair_copy().wait_send()
    for i in range(shared):

        @pl.when(homes(side, i) != m)
        def _():
            part_copy(i).wait_send()

    for d in range(1, members):
        sh_copy(d).wait_send()
    lax.fori_loop(SUBS // 2, SUBS, before_last_update, 0)

    def last(j, carry):
        phase(j, members - 1, forward=False)
        return carry

    lax.fori_loop(0, SUBS, last, 0)

    def finish(b, carry):
        at = pl.multiple_of(b * BLOCK, BLOCK)
        out_ref[pl.ds(at, BLOCK), :] = acc[pl.ds(at, BLOCK), :].astype(out_ref.dtype)
        return carry

    lax.fori_loop(0, blocks_here, finish, 0)

    for r in range(RINGS):
        whole = gat.at[r, :, pl.ds(0, members - 1)]
        pltpu.make_async_remote_copy(
            src_ref=whole,
            dst_ref=whole,
            send_sem=ring_send.at[r],
            recv_sem=ring_recv.at[r, 0, 0],
            device_id={"tp": nexts[r]},
            device_id_type=pl.DeviceIdType.MESH,
        ).wait_send()


def local(tokens, frozen_weight, down_weight, up_weight, adapter_storage_slot, adapter_of_block):
    groups = lax.axis_size("grp")
    members = lax.axis_size("tp")
    rows, width = tokens.shape
    rank, down_width = down_weight.shape[1:]
    columns = frozen_weight.shape[1]
    chunk = width // (RINGS * SUBS)
    bf16, f32 = jnp.bfloat16, jnp.float32
    hbm_spec = pl.BlockSpec(memory_space=pltpu.HBM)
    dma = pltpu.SemaphoreType.DMA
    return pl.pallas_call(
        kernel,
        out_shape=jax.ShapeDtypeStruct((members * rows, columns), bf16),
        in_specs=[hbm_spec, hbm_spec, hbm_spec, hbm_spec, hbm_spec, hbm_spec],
        out_specs=pl.BlockSpec(memory_space=pltpu.VMEM),
        scratch_shapes=[
            pltpu.SMEM(adapter_storage_slot.shape, jnp.int32),
            pltpu.SMEM(adapter_of_block.shape, jnp.int32),
            pltpu.VMEM((RINGS, SUBS, members, rows, chunk), bf16),
            pltpu.VMEM((CHUNKS, chunk, columns), bf16),
            pltpu.VMEM(down_weight.shape, bf16),
            pltpu.VMEM(up_weight.shape, bf16),
            pltpu.VMEM((groups, rank, down_width), bf16),
            pltpu.VMEM((groups, rank, columns), bf16),
            pltpu.VMEM((groups, rank, down_width), bf16),
            pltpu.VMEM((groups, rank, columns), bf16),
            pltpu.VMEM((members * rows, columns), f32),
            pltpu.VMEM((members // 2, rows // 2, 2 * rank), f32),
            pltpu.VMEM((members // 2, rows // 2, 2 * rank), f32),
            pltpu.VMEM((members // 2, rows // 2, 2 * rank), f32),
            pltpu.VMEM((members, rows // 2, 2 * rank), f32),
            pltpu.VMEM((rows // 2, 2 * rank), bf16),
            pltpu.VMEM((members, rows // 2, 2 * rank), bf16),
            dma((RINGS, SUBS)),
            dma((CHUNKS,)),
            dma((4,)),
            dma((RINGS,)),
            dma((RINGS, SUBS, members)),
            dma((groups,)),
            dma((groups,)),
            dma((groups,)),
            dma((groups,)),
            dma((2,)),
            dma((members,)),
            dma((members,)),
            dma((members,)),
            dma((members,)),
            pltpu.SemaphoreType.REGULAR((3,)),
        ],
        compiler_params=pltpu.CompilerParams(
            collective_id=0, has_side_effects=True, vmem_limit_bytes=42 << 20
        ),
        cost_estimate=pl.CostEstimate(
            flops=2 * members * rows * width * columns,
            bytes_accessed=2 * width * columns + 2 * members * rows * columns,
            transcendentals=0,
        ),
        name="projection",
    )(
        *[
            pltpu.with_memory_space_constraint(a, pltpu.HBM)
            for a in (adapter_storage_slot, adapter_of_block, tokens, frozen_weight, down_weight, up_weight)
        ]
    )


def solution(mesh):
    placed = (
        P(("grp", "tp"), None),
        P(None, "tp"),
        P("grp", None, "tp"),
        P("grp", None, "tp"),
        P(),
        P(),
    )
    return jax.shard_map(
        local, mesh=mesh, in_specs=placed, out_specs=P("grp", "tp"), check_vma=False
    )
```
